32 devices in a mesh: layer: 8 (over y, x, core), dp: 4 (over z).
Axes of the slice: x: 2, y: 2, z: 4, core: 2. Of those that a mesh axis runs over, the one named last changes fastest.
Arguments:
- images: float32 [8, 16, 16, 128], P('dp'), may hold values from -6 to 6
- weights: bfloat16 [32, 3, 3, 128, 128], P('layer'), may hold values from -0.1875 to 0.1875
- biases: float32 [32, 128], P('layer'), may hold values from -3 to 3
- end_grad: float32 [8, 16, 16, 128], P('dp'), may hold values from -6 to 6
Outputs:
- interval_ends: float32 [8, 8, 16, 16, 128], P('layer', 'dp')
- start_adjoint: float32 [8, 8, 16, 16, 128], P('layer', 'dp')
- weight_grad: float32 [32, 3, 3, 128, 128], P('layer')
- bias_grad: float32 [32, 128], P('layer')
The draws below stay inside these ranges and needn't reach their ends.
All inputs are finite; a program needn't handle non-finite values.
Results may differ from the reference program's by a relative error of at most 0.012.
The reference program's roundings to bfloat16 on the way count: a program that leaves them out, or rounds other values in their place, can miss the bound.
Values sent between devices are 32-bit elements; how exact they have to be, the bound alone decides.
A program may use at most 128 MiB of HBM per device.

```python
import jax
import jax.numpy as jnp
from jax import lax

C = 128
H = 16
W = 16
BLK = 4
LAYERS = 32
IMAGES = 8
N_LAYER = 8


def steps_of(own_key, shape, split, least, high):
    loudness = 1.0
    for axis_at, blocks in split:
        draws = jax.random.uniform(jax.random.fold_in(jax.random.fold_in(own_key, 6), axis_at), (blocks,), jnp.float32, least / len(split), high / len(split))
        loudness = loudness * jnp.repeat(jnp.exp(draws), shape[axis_at] // blocks).reshape((-1,) + (1,) * (len(shape) - 1 - axis_at))
    return loudness


def noise(stream_key, shape, spread, limit, cuts=(), kind=jnp.bfloat16):
    loudness = steps_of(stream_key, shape, cuts, -0.22, 0.18) if cuts else 1.0
    drawn = jax.random.normal(stream_key, shape, jnp.float32) * spread * loudness
    return jnp.minimum(jnp.maximum(drawn, -limit), limit).astype(kind)


def setup_inputs(seed: int = 0) -> dict:
    arg_keys = jax.random.split(jax.random.key(seed), 5)
    return {
        "images": noise(arg_keys[0], (IMAGES, H, W, C), 1.0, 6.0, ((0, 4),), jnp.float32),
        "weights": noise(arg_keys[1], (LAYERS, 3, 3, C, C), (9 * C) ** -0.5, 0.1875, ((0, 8),)),
        "biases": noise(arg_keys[2], (LAYERS, C), 0.5, 3.0, ((0, 8),), jnp.float32),
        "end_grad": noise(arg_keys[3], (IMAGES, H, W, C), 1.0, 6.0, ((0, 4),), jnp.float32),
    }


step_size = 0.25
conv_layout = ('NHWC', 'HWIO', 'NHWC')

def convolve(states, kernel):
    return lax.conv_general_dilated(states.astype(jnp.bfloat16), kernel, (1, 1), 'SAME', dimension_numbers=conv_layout, preferred_element_type=jnp.float32)

def advance(states, weights, biases):
    inputs = []
    slopes = []
    for index in range(weights.shape[0]):
        preact = convolve(states, weights[index]) + biases[index]
        activation = jnp.tanh(preact)
        inputs.append(states.astype(jnp.bfloat16))
        slopes.append(activation)
        states = states + step_size * activation
    return (states, inputs, slopes)

def retreat(adjoint, transposed, slopes):
    for index in reversed(range(len(slopes))):
        change = step_size * (1.0 - slopes[index] * slopes[index]) * adjoint
        adjoint = adjoint + convolve(change, transposed[index])
    return adjoint

def kernel_grad(inputs_low, change_low):
    padded = jnp.pad(inputs_low, ((0, 0), (1, 1), (1, 1), (0, 0))).astype(jnp.float32)
    change_wide = change_low.astype(jnp.float32)
    height = change_low.shape[1]
    width = change_low.shape[2]
    taps = []
    for row_at in range(3):
        line = []
        for col_at in range(3):
            window = padded[:, row_at:row_at + height, col_at:col_at + width, :]
            line.append(jnp.einsum('bhwc,bhwd->cd', window, change_wide))
        taps.append(jnp.stack(line))
    return jnp.stack(taps)

def finish(adjoint, transposed, inputs, slopes):
    kernels = []
    offsets = []
    for index in reversed(range(len(slopes))):
        change = step_size * (1.0 - slopes[index] * slopes[index]) * adjoint
        change_low = change.astype(jnp.bfloat16)
        kernels.append(kernel_grad(inputs[index], change_low))
        offsets.append(lax.optimization_barrier(jnp.sum(change, axis=(0, 1, 2))))
        adjoint = adjoint + convolve(change_low, transposed[index])
    return (adjoint, jnp.stack(kernels[::-1]), jnp.stack(offsets[::-1]))

def coarse_chain(matrices, residues, backward):

    def advance_error(carried, pieces):
        matrix, residue = pieces
        return (jnp.einsum('bhwc,cd->bhwd', carried, matrix, precision=lax.Precision.HIGHEST) + residue, carried)
    _, result = lax.scan(advance_error, jnp.zeros_like(residues[0]), (matrices, residues), reverse=backward)
    return result

def apply_map(field, matrix):
    return jnp.einsum('bhwc,cd->bhwd', field, matrix, precision=lax.Precision.HIGHEST)

def reference(images, weights, biases, end_grad):
    kernels = weights.reshape(N_LAYER, BLK, 3, 3, C, C)
    offsets = biases.reshape(N_LAYER, BLK, C)
    transposed = jnp.swapaxes(jnp.flip(kernels, (2, 3)), 4, 5)
    matrices = jnp.eye(C, dtype=jnp.float32) + step_size * lax.optimization_barrier(jnp.sum(kernels[:, :, 1, 1].astype(jnp.float32), axis=1))
    guess = jax.vmap(apply_map, in_axes=(None, 0))(images, matrices)
    starts = jnp.concatenate([images[None], guess[:-1]], axis=0)
    relaxed, _, _ = jax.vmap(advance, in_axes=(0, 0, 0))(starts, kernels, offsets)
    error = coarse_chain(matrices, relaxed - guess, False)
    corrected = starts + error
    interval_ends, inputs, slopes = jax.vmap(advance, in_axes=(0, 0, 0))(corrected, kernels, offsets)
    back = jax.vmap(apply_map, in_axes=(None, 0))(end_grad, jnp.swapaxes(matrices, 1, 2))
    ends_adj = jnp.concatenate([back[1:], end_grad[None]], axis=0)
    again = jax.vmap(retreat, in_axes=(0, 0, 0))(ends_adj, transposed, slopes)
    adj_error = coarse_chain(jnp.swapaxes(matrices, 1, 2), again - back, True)
    start_adjoint, kernel_sums, offset_sums = jax.vmap(finish, in_axes=(0, 0, 0, 0))(ends_adj + adj_error, transposed, inputs, slopes)
    divisor = 1.0 / images.shape[0]
    weight_grad = kernel_sums.reshape(LAYERS, 3, 3, C, C) * divisor
    bias_grad = offset_sums.reshape(LAYERS, C) * divisor
    return (interval_ends, start_adjoint, weight_grad, bias_grad)
```

```python
import functools

import jax
import jax.numpy as jnp
from jax import lax
from jax.experimental import pallas as pl
from jax.experimental.pallas import tpu as pltpu
from jax.sharding import PartitionSpec as P

step_size = 0.25
MESH = pl.DeviceIdType.MESH
low = jnp.bfloat16


def dot(a, b, contract=((1,), (0,))):
    return lax.dot_general(a, b, (contract, ((), ())), preferred_element_type=jnp.float32)


NN = ((1,), (0,))
NT = ((1,), (1,))
TN = ((0,), (0,))


def kernel(
    dims,
    images_in,
    weights_in,
    biases_in,
    end_grad_in,
    both_out,
    wg_out,
    bg_out,
    images,
    weights,
    biases,
    end_grad,
    load_sems,
    ahead_pair,
    ahead_edge,
    back_pair,
    back_edge,
    maps,
    states_low,
    slopes,
    states_all,
    adj_all,
    residue,
    gathered,
    spread,
    error,
    map_send,
    map_recv,
    hand_send,
    out_send,
    out_recv,
    back_send,
    back_recv,
    right_send,
    left_send,
    line_recv,
):
    groups, parts, count, height, width, images_all = dims
    rows, channels = images_in.shape
    blocks = weights_in.shape[0]
    share = rows // groups
    me = lax.axis_index("layer")
    z = lax.axis_index("dp")
    not_first = z > 0
    not_last = z < parts - 1

    def others(body):
        def step(ahead, _):
            body(ahead, lax.rem(me + ahead, groups))
            return 0

        lax.fori_loop(1, groups, step, 0)

    loads = [
        pltpu.make_async_copy(source, target, load_sems.at[i])
        for i, (source, target) in enumerate(
            ((weights_in, weights), (images_in, images), (biases_in, biases), (end_grad_in, end_grad))
        )
    ]
    for load in loads:
        load.start()
    barrier = pltpu.get_barrier_semaphore()
    others(lambda ahead, to: pl.semaphore_signal(barrier, inc=1, device_id={"layer": to}, device_id_type=MESH))

    @pl.when(not_first)
    def _():
        pl.semaphore_signal(barrier, inc=1, device_id={"dp": z - 1}, device_id_type=MESH)

    @pl.when(not_last)
    def _():
        pl.semaphore_signal(barrier, inc=1, device_id={"dp": z + 1}, device_id_type=MESH)

    loads[0].wait()
    centre = slice(4 * channels, 5 * channels)
    total = weights[0, centre, :].astype(jnp.float32)
    for n in range(1, blocks):
        total = total + weights[n, centre, :].astype(jnp.float32)
    maps[me] = step_size * total

    neighbours = jnp.where(not_first, 1, 0) + jnp.where(not_last, 1, 0)
    pl.semaphore_wait(barrier, groups - 1 + neighbours)

    def map_copy(slot, to):
        return pltpu.make_async_remote_copy(
            src_ref=maps.at[slot],
            dst_ref=maps.at[slot],
            send_sem=map_send.at[to],
            recv_sem=map_recv.at[slot],
            device_id={"layer": to},
            device_id_type=MESH,
        )

    last = groups - 1
    after = lax.rem(me + 1, groups)
    before = lax.rem(me + last, groups)
    pair = 2 if groups % 2 == 0 else 1
    partner = me + 1 - 2 * lax.rem(me, 2) if pair == 2 else me

    def same_side(body):
        def step(ahead, _):
            body(lax.rem(me + pair * ahead, groups))
            return 0

        lax.fori_loop(1, groups // pair, step, 0)

    map_copy(me, after).start()
    if pair == 2:

        @pl.when(partner != after)
        def _():
            map_copy(me, partner).start()

    def send_map(to):
        if pair == 1:

            @pl.when(to != after)
            def _():
                map_copy(me, to).start()

        else:
            map_copy(me, to).start()

    same_side(send_map)

    def hand_copy(slot):
        return pltpu.make_async_remote_copy(
            src_ref=maps.at[slot],
            dst_ref=maps.at[slot],
            send_sem=hand_send.at[slot],
            recv_sem=map_recv.at[slot],
            device_id={"layer": partner},
            device_id_type=MESH,
        )

    def is_handed(slot):
        return lax.rem(slot + 1, groups) != partner

    def hand_on(slot):
        @pl.when((slot != before) | (me == 0))
        def _():
            map_copy(slot, me).wait_recv()

        if pair == 2:

            @pl.when(is_handed(slot))
            def _():
                hand_copy(slot).start()

    for load in loads[1:]:
        load.wait()

    def prepare(n, _):
        def tap(i, j):
            at = (3 * i + j) * channels
            return weights[n, at : at + channels, :]

        def spot(i):
            return slice(i * channels, (i + 1) * channels)

        nothing = jnp.zeros((channels, channels), low)
        for i in range(3):
            for j in range(2):
                ahead_pair[n, spot(j), spot(i)] = tap(i, j)
                back_pair[n, spot(i), spot(j)] = tap(2 - i, 2 - j)
        ahead_edge[n, spot(0), spot(0)] = tap(0, 2)
        ahead_edge[n, spot(0), spot(1)] = nothing
        ahead_edge[n, spot(1), spot(0)] = tap(1, 2)
        ahead_edge[n, spot(1), spot(1)] = tap(2, 2)
        back_edge[n, spot(0), spot(0)] = tap(2, 0)
        back_edge[n, spot(1), spot(0)] = nothing
        back_edge[n, spot(0), spot(1)] = tap(1, 0)
        back_edge[n, spot(1), spot(1)] = tap(0, 0)
        wg_out[n] = jnp.zeros(wg_out.shape[1:], jnp.float32)
        return 0

    lax.fori_loop(0, blocks, prepare, 0)
    bg_out[...] = jnp.zeros(bg_out.shape, jnp.float32)

    column = lax.rem(lax.broadcasted_iota(jnp.int32, (rows, channels), 0), width)

    area = height * width

    def down(field):
        blank = jnp.zeros((width, field.shape[1]), field.dtype)
        lines = []
        for at in range(0, field.shape[0], area):
            lines += [blank, field[at : at + area - width]]
        return jnp.concatenate(lines, axis=0)

    def up(field):
        blank = jnp.zeros((width, field.shape[1]), field.dtype)
        lines = []
        for at in range(0, field.shape[0], area):
            lines += [field[at + width : at + area], blank]
        return jnp.concatenate(lines, axis=0)

    def sides(field):
        size = field.shape[0]
        place = column[:size]
        left = jnp.where(place == 0, 0.0, pltpu.roll(field, 1, 0))
        right = jnp.where(place == width - 1, 0.0, pltpu.roll(field, size - 1, 0))
        return left.astype(low), field.astype(low), right.astype(low)

    def combine(three, pair_weights, edge_weights, contract):
        left, middle, right = three
        a = dot(jnp.concatenate([left, middle], axis=1), pair_weights, contract)
        b = dot(jnp.concatenate([down(right), right], axis=1), edge_weights, contract)
        c = channels
        return a[:, c : 2 * c] + b[:, :c] + down(a[:, :c]) + up(a[:, 2 * c :] + b[:, c:])

    def conv(n, field):
        return combine(sides(field), ahead_pair[n], ahead_edge[n], NN)

    def apply_map(field, slot):
        return field + dot(field.astype(low), maps[slot].astype(low))

    def apply_flipped(field, slot):
        return field + dot(field.astype(low), maps[slot].astype(low), NT)

    def split(field):
        return tuple(field[at : at + area] for at in range(0, field.shape[0], area))

    def join(fields):
        return jnp.concatenate(fields, axis=0)

    def span(i):
        return slice(i * area, (i + 1) * area)

    def advance(n, states):
        return tuple(
            state + step_size * jnp.tanh(conv(n, state) + biases[pl.ds(n, 1), :]) for state in states
        )

    def trajectory(part, state):
        def step(n, states):
            after = []
            for i, state in enumerate(states):
                states_low[n, part, span(i)] = state.astype(low)
                activation = jnp.tanh(conv(n, state) + biases[pl.ds(n, 1), :])
                slopes[n, part, span(i)] = activation
                after.append(state + step_size * activation)
            return tuple(after)

        return join(lax.fori_loop(0, blocks, step, split(state), unroll=4))

    def change_of(n, part, adjoint, i):
        slope = slopes[n, part, span(i)]
        return step_size * (1.0 - slope * slope) * adjoint

    def retreat(part, adjoint):
        def step(i, adjoints):
            n = blocks - 1 - i
            return tuple(
                adjoint + combine(sides(change_of(n, part, adjoint, at)), back_pair[n], back_edge[n], NT)
                for at, adjoint in enumerate(adjoints)
            )

        return join(lax.fori_loop(0, blocks, step, split(adjoint), unroll=4))

    divisor = 1.0 / images_all

    def sweep(part, adjoint, first=0):
        def step(i, adjoints):
            n = blocks - 1 - i
            after = []
            spots = []
            for at, adjoint in enumerate(adjoints):
                change = change_of(n, part, adjoint, first + at)
                bg_out[pl.ds(n, 1), :] += jnp.sum(change, axis=0, keepdims=True) * divisor
                three = sides(change)
                after.append(adjoint + combine(three, back_pair[n], back_edge[n], NT))
                line = jnp.concatenate(three, axis=1)
                spots.append(jnp.concatenate([down(line), line, up(line)], axis=1))
            used = states_low[n, part, first * area : (first + len(spots)) * area]
            grads = dot(used, join(spots), TN) * divisor
            for tap in range(9):
                wg_out[n, (8 - tap) * channels : (9 - tap) * channels, :] += grads[
                    :, tap * channels : (tap + 1) * channels
                ]
            return tuple(after)

        return join(lax.fori_loop(0, blocks, step, split(adjoint), unroll=4))

    def rows_of(slot):
        return pl.ds(pl.multiple_of(slot * share, share), share)

    def out_copy(phase, source, to):
        return pltpu.make_async_remote_copy(
            src_ref=residue.at[phase, rows_of(to)],
            dst_ref=gathered.at[phase, source],
            send_sem=out_send.at[phase, to],
            recv_sem=out_recv.at[phase, source],
            device_id={"layer": to},
            device_id_type=MESH,
        )

    def back_copy(phase, source, to):
        return pltpu.make_async_remote_copy(
            src_ref=spread.at[phase, to],
            dst_ref=error.at[phase, rows_of(source)],
            send_sem=back_send.at[phase, to],
            recv_sem=back_recv.at[phase, source],
            device_id={"layer": to},
            device_id_type=MESH,
        )

    def chain_start(phase, value):
        residue[phase] = value
        others(lambda ahead, to: out_copy(phase, me, to).start())
        gathered[phase, me] = residue[phase, rows_of(me)]

    def chain_scan(phase):
        def step(i, carried):
            k = i if phase == 0 else groups - 1 - i

            @pl.when(k != me)
            def _():
                spread[phase, k] = carried
                back_copy(phase, me, k).start()
                out_copy(phase, k, me).wait_recv()

            @pl.when(k == me)
            def _():
                error[phase, rows_of(me)] = carried

            mapped = apply_map(carried, k) if phase == 0 else apply_flipped(carried, k)
            return mapped + gathered[phase, k]

        lax.fori_loop(0, groups, step, jnp.zeros((share, channels), jnp.float32))

    def chain_finish(phase):
        others(lambda ahead, to: back_copy(phase, to, me).wait_recv())
        return error[phase]

    line = (states_all, adj_all)

    piece = rows // count

    def line_copy(which, block, part, to, sends):
        where = line[which].at[block, part * piece : (part + 1) * piece]
        return pltpu.make_async_remote_copy(
            src_ref=where,
            dst_ref=where,
            send_sem=sends.at[which, block, part],
            recv_sem=line_recv.at[which, block, part],
            device_id={"dp": to},
            device_id_type=MESH,
        )

    def go_right(which, block, part):
        @pl.when(not_last)
        def _():
            line_copy(which, block, part, z + 1, right_send).start()

    def go_left(which, block, part):
        @pl.when(not_first)
        def _():
            line_copy(which, block, part, z - 1, left_send).start()

    def line_start(which):
        for part in range(count):
            go_right(which, z, part)
            go_left(which, z, part)

    def line_round(which, away, pieces=range(count)):
        for part in pieces:

            @pl.when(z - away >= 0)
            def _():
                line_copy(which, z - away, part, z, right_send).wait_recv()
                go_right(which, z - away, part)

            @pl.when(z + away < parts)
            def _():
                line_copy(which, z + away, part, z, left_send).wait_recv()
                go_left(which, z + away, part)

    def nth_other(i):
        back_side = parts - 1 - z
        paired = jnp.where(z < back_side, z, back_side)
        near = i // 2 + 1
        near_part = jnp.where(i % 2 == 0, z - near, z + near)
        far = i - paired + 1
        far_part = jnp.where(z > back_side, z - far, z + far)
        return jnp.where(i < 2 * paired, near_part, far_part)

    def other_trajectory(i):
        part = nth_other(i)
        trajectory(part, states_all[part])

    start_image = images[...]

    @pl.when(me != 0)
    def _():
        map_copy(before, me).wait_recv()

    starts = jnp.where(me == 0, start_image, apply_map(start_image, jnp.where(me == 0, me, before)))
    relaxed = join(lax.fori_loop(0, blocks, advance, split(starts), unroll=4))
    chain_start(0, relaxed - apply_map(start_image, me))

    same_side(hand_on)

    def wait_map(ahead, source):
        @pl.when((lax.rem(source - me + groups, pair) != 0) & ((source != before) | (me == 0)))
        def _():
            map_copy(source, me).wait_recv()

    if pair == 2:
        others(wait_map)
    end = end_grad[...]
    ends_adj = jnp.where(me == last, end, apply_flipped(end, after))
    back = apply_flipped(end, me)
    chain_scan(0)
    corrected = starts + chain_finish(0)
    states_all[z] = corrected
    line_start(0)
    both_out[0] = trajectory(z, corrected)

    chain_start(1, retreat(z, ends_adj) - back)
    if parts > 1:
        line_round(0, 1)
        other_trajectory(0)
    chain_scan(1)
    if parts > 2:
        line_round(0, 2)
        other_trajectory(1)
    adjoint = ends_adj + chain_finish(1)
    adj_all[z] = adjoint
    line_start(1)
    both_out[1] = sweep(z, adjoint)
    for i in range(2, parts - 1):
        line_round(0, i + 1)
        other_trajectory(i)
    for i in range(parts - 2):
        line_round(1, i + 1)
        part = nth_other(i)
        sweep(part, adj_all[part])
    if parts > 1:
        part = nth_other(parts - 2)
        for i in range(count):
            line_round(1, parts - 1, (i,))
            sweep(part, adj_all[part, i * piece : (i + 1) * piece], i)

    def map_sent(to):
        if pair == 1:

            @pl.when(to != after)
            def _():
                map_copy(me, to).wait_send()

        else:
            map_copy(me, to).wait_send()

            @pl.when(is_handed(to))
            def _():
                hand_copy(to).wait_send()

    map_copy(me, after).wait_send()
    if pair == 2:

        @pl.when(partner != after)
        def _():
            map_copy(me, partner).wait_send()

    same_side(map_sent)

    def sent(ahead, to):
        for phase in range(2):
            out_copy(phase, me, to).wait_send()
            back_copy(phase, me, to).wait_send()

    others(sent)
    for which in range(2):
        for away in range(parts):

            @pl.when((z - away >= 0) & not_last)
            def _():
                for part in range(count):
                    line_copy(which, z - away, part, z + 1, right_send).wait_send()

            @pl.when((z + away < parts) & not_first)
            def _():
                for part in range(count):
                    line_copy(which, z + away, part, z - 1, left_send).wait_send()


def shards(images, weights, biases, end_grad):
    groups = lax.axis_size("layer")
    parts = lax.axis_size("dp")
    count, height, width, channels = images.shape
    blocks = weights.shape[0]
    rows = count * height * width
    dims = (groups, parts, count, height, width, count * parts)
    f32 = jnp.float32
    share = rows // groups
    dma = pltpu.SemaphoreType.DMA
    vmem = pl.BlockSpec(memory_space=pltpu.VMEM)
    both, wg, bg = pl.pallas_call(
        functools.partial(kernel, dims),
        out_shape=(
            pltpu.VMEM((2, rows, channels), f32),
            pltpu.VMEM((blocks, 9 * channels, channels), f32),
            pltpu.VMEM((blocks, channels), f32),
        ),
        in_specs=[pl.BlockSpec(memory_space=pltpu.HBM)] * 4,
        out_specs=(vmem,) * 3,
        scratch_shapes=[
            pltpu.VMEM((rows, channels), f32),
            pltpu.VMEM((blocks, 9 * channels, channels), low),
            pltpu.VMEM((blocks, channels), f32),
            pltpu.VMEM((rows, channels), f32),
            dma((4,)),
            pltpu.VMEM((blocks, 2 * channels, 3 * channels), low),
            pltpu.VMEM((blocks, 2 * channels, 2 * channels), low),
            pltpu.VMEM((blocks, 3 * channels, 2 * channels), low),
            pltpu.VMEM((blocks, 2 * channels, 2 * channels), low),
            pltpu.VMEM((groups, channels, channels), f32),
            pltpu.VMEM((blocks, parts, rows, channels), low),
            pltpu.VMEM((blocks, parts, rows, channels), f32),
            pltpu.VMEM((parts, rows, channels), f32),
            pltpu.VMEM((parts, rows, channels), f32),
            pltpu.VMEM((2, rows, channels), f32),
            pltpu.VMEM((2, groups, share, channels), f32),
            pltpu.VMEM((2, groups, share, channels), f32),
            pltpu.VMEM((2, rows, channels), f32),
            dma((groups,)),
            dma((groups,)),
            dma((groups,)),
            dma((2, groups)),
            dma((2, groups)),
            dma((2, groups)),
            dma((2, groups)),
            dma((2, parts, count)),
            dma((2, parts, count)),
            dma((2, parts, count)),
        ],
        compiler_params=pltpu.CompilerParams(
            collective_id=0, has_side_effects=True, vmem_limit_bytes=61 << 20
        ),
    )(
        images.reshape(rows, channels),
        weights.reshape(blocks, 9 * channels, channels),
        biases,
        end_grad.reshape(rows, channels),
    )
    shape = (1,) + images.shape
    return (both[0].reshape(shape), both[1].reshape(shape), wg.reshape(weights.shape), bg)


def solution(mesh):
    in_specs = (
        P("dp", None, None, None),
        P("layer", None, None, None, None),
        P("layer", None),
        P("dp", None, None, None),
    )
    out_specs = (
        P("layer", "dp", None, None, None),
        P("layer", "dp", None, None, None),
        P("layer", None, None, None, None),
        P("layer", None),
    )
    return jax.shard_map(shards, mesh=mesh, in_specs=in_specs, out_specs=out_specs, check_vma=False)
```

```python
import functools

import jax
import jax.numpy as jnp
from jax import lax
from jax.experimental import pallas as pl
from jax.experimental.pallas import tpu as pltpu
from jax.sharding import PartitionSpec as P

step_size = 0.25
MESH = pl.DeviceIdType.MESH
low = jnp.bfloat16


def dot(a, b, contract=((1,), (0,))):
    return lax.dot_general(a, b, (contract, ((), ())), preferred_element_type=jnp.float32)


NN = ((1,), (0,))
NT = ((1,), (1,))
TN = ((0,), (0,))


def kernel(
    dims,
    images_in,
    weights_in,
    biases_in,
    end_grad_in,
    both_out,
    wg_out,
    bg_out,
    weights,
    biases,
    end_grad,
    load_sems,
    ahead_pair,
    ahead_edge,
    back_pair,
    back_edge,
    maps,
    states_low,
    slopes,
    states_all,
    adj_all,
    residue,
    gathered,
    spread,
    error,
    map_send,
    map_recv,
    hand_send,
    out_send,
    out_recv,
    back_send,
    back_recv,
    right_send,
    left_send,
    line_recv,
    part_images,
    other_starts,
    other_fine,
    handoff,
    pass_send,
    pass_recv,
    part_grads,
    share_send,
    share_recv,
    spread_send,
    spread_recv,
):
    groups, parts, count, height, width, images_all = dims
    rows, channels = images_in.shape
    blocks = weights_in.shape[0]
    share = rows // groups
    me = lax.axis_index("layer")
    z = lax.axis_index("dp")
    not_first = z > 0
    not_last = z < parts - 1

    def others(body):
        def step(ahead, _):
            body(ahead, lax.rem(me + ahead, groups))
            return 0

        lax.fori_loop(1, groups, step, 0)

    loads = [
        pltpu.make_async_copy(source, target, load_sems.at[i])
        for i, (source, target) in enumerate(
            ((weights_in, weights), (images_in, part_images.at[z]), (biases_in, biases), (end_grad_in, end_grad))
        )
    ]
    for load in loads:
        load.start()
    barrier = pltpu.get_barrier_semaphore()
    others(lambda ahead, to: pl.semaphore_signal(barrier, inc=1, device_id={"layer": to}, device_id_type=MESH))

    for ahead in range(1, parts):
        pl.semaphore_signal(
            barrier, inc=1, device_id={"dp": lax.rem(z + ahead, parts)}, device_id_type=MESH
        )

    loads[0].wait()
    centre = slice(4 * channels, 5 * channels)
    total = weights[0, centre, :].astype(jnp.float32)
    for n in range(1, blocks):
        total = total + weights[n, centre, :].astype(jnp.float32)
    maps[me] = step_size * total

    pl.semaphore_wait(barrier, groups - 1 + parts - 1)

    def map_copy(slot, to):
        return pltpu.make_async_remote_copy(
            src_ref=maps.at[slot],
            dst_ref=maps.at[slot],
            send_sem=map_send.at[to],
            recv_sem=map_recv.at[slot],
            device_id={"layer": to},
            device_id_type=MESH,
        )

    last = groups - 1
    after = lax.rem(me + 1, groups)
    before = lax.rem(me + last, groups)
    pair = 2 if groups % 2 == 0 else 1
    partner = me + 1 - 2 * lax.rem(me, 2) if pair == 2 else me

    def same_side(body):
        def step(ahead, _):
            body(lax.rem(me + pair * ahead, groups))
            return 0

        lax.fori_loop(1, groups // pair, step, 0)

    map_copy(me, after).start()
    if pair == 2:

        @pl.when(partner != after)
        def _():
            map_copy(me, partner).start()

    def send_map(to):
        if pair == 1:

            @pl.when(to != after)
            def _():
                map_copy(me, to).start()

        else:
            map_copy(me, to).start()

    same_side(send_map)

    def hand_copy(slot):
        return pltpu.make_async_remote_copy(
            src_ref=maps.at[slot],
            dst_ref=maps.at[slot],
            send_sem=hand_send.at[slot],
            recv_sem=map_recv.at[slot],
            device_id={"layer": partner},
            device_id_type=MESH,
        )

    def is_handed(slot):
        return lax.rem(slot + 1, groups) != partner

    def hand_on(slot):
        @pl.when((slot != before) | (me == 0))
        def _():
            map_copy(slot, me).wait_recv()

        if pair == 2:

            @pl.when(is_handed(slot))
            def _():
                hand_copy(slot).start()

    for load in loads[1:]:
        load.wait()

    lead = lax.rem(me, 2) == 0

    def rows_of(slot):
        return pl.ds(pl.multiple_of(slot * share, share), share)

    def other_planes(body, who=True):
        for away in range(1, parts):

            @pl.when(who & (z + away < parts))
            def _():
                body(z + away)

            @pl.when(who & (z - away >= 0))
            def _():
                body(z - away)

    def share_copy(part, to):
        return pltpu.make_async_remote_copy(
            src_ref=end_grad.at[rows_of(me)],
            dst_ref=part_grads.at[part, rows_of(me)],
            send_sem=share_send.at[to],
            recv_sem=share_recv.at[part],
            device_id={"dp": to},
            device_id_type=MESH,
        )

    def spread_copy(part, source, to):
        return pltpu.make_async_remote_copy(
            src_ref=part_grads.at[part, rows_of(source)],
            dst_ref=part_grads.at[part, rows_of(source)],
            send_sem=spread_send.at[part, to // 2],
            recv_sem=spread_recv.at[part, source],
            device_id={"layer": to},
            device_id_type=MESH,
        )

    def odd_others(body):
        def step(i, _):
            to = 2 * i + 1

            @pl.when(to != me)
            def _():
                body(to)

            return 0

        lax.fori_loop(0, groups // 2, step, 0)

    other_planes(lambda to: share_copy(z, to).start(), me >= 0)

    line = (states_all, adj_all, part_images)
    piece = rows // count

    def line_copy(which, block, part, to, sends):
        where = line[which].at[block, part * piece : (part + 1) * piece]
        return pltpu.make_async_remote_copy(
            src_ref=where,
            dst_ref=where,
            send_sem=sends.at[which, block, part],
            recv_sem=line_recv.at[which, block, part],
            device_id={"dp": to},
            device_id_type=MESH,
        )

    def go_right(which, block, part):
        @pl.when(not_last)
        def _():
            line_copy(which, block, part, z + 1, right_send).start()

    def go_left(which, block, part):
        @pl.when(not_first)
        def _():
            line_copy(which, block, part, z - 1, left_send).start()

    def takes(which):
        return jnp.logical_not(lead) if which == 1 else lead

    def line_start(which):
        @pl.when(takes(which))
        def _():
            for part in range(count):
                go_right(which, z, part)
                go_left(which, z, part)

    def line_round(which, away, pieces=range(count)):
        for part in pieces:

            @pl.when(takes(which) & (z - away >= 0))
            def _():
                line_copy(which, z - away, part, z, right_send).wait_recv()
                go_right(which, z - away, part)

            @pl.when(takes(which) & (z + away < parts))
            def _():
                line_copy(which, z + away, part, z, left_send).wait_recv()
                go_left(which, z + away, part)

    line_start(2)

    def prepare(n, _):
        def tap(i, j):
            at = (3 * i + j) * channels
            return weights[n, at : at + channels, :]

        def spot(i):
            return slice(i * channels, (i + 1) * channels)

        nothing = jnp.zeros((channels, channels), low)
        for i in range(3):
            for j in range(2):
                ahead_pair[n, spot(j), spot(i)] = tap(i, j)
                back_pair[n, spot(i), spot(j)] = tap(2 - i, 2 - j)
        ahead_edge[n, spot(0), spot(0)] = tap(0, 2)
        ahead_edge[n, spot(0), spot(1)] = nothing
        ahead_edge[n, spot(1), spot(0)] = tap(1, 2)
        ahead_edge[n, spot(1), spot(1)] = tap(2, 2)
        back_edge[n, spot(0), spot(0)] = tap(2, 0)
        back_edge[n, spot(1), spot(0)] = nothing
        back_edge[n, spot(0), spot(1)] = tap(1, 0)
        back_edge[n, spot(1), spot(1)] = tap(0, 0)
        wg_out[n] = jnp.zeros(wg_out.shape[1:], jnp.float32)
        return 0

    lax.fori_loop(0, blocks, prepare, 0)
    bg_out[...] = jnp.zeros(bg_out.shape, jnp.float32)

    column = lax.rem(lax.broadcasted_iota(jnp.int32, (rows, channels), 0), width)

    area = height * width

    def down(field):
        blank = jnp.zeros((width, field.shape[1]), field.dtype)
        lines = []
        for at in range(0, field.shape[0], area):
            lines += [blank, field[at : at + area - width]]
        return jnp.concatenate(lines, axis=0)

    def up(field):
        blank = jnp.zeros((width, field.shape[1]), field.dtype)
        lines = []
        for at in range(0, field.shape[0], area):
            lines += [field[at + width : at + area], blank]
        return jnp.concatenate(lines, axis=0)

    def sides(field):
        size = field.shape[0]
        place = column[:size]
        left = jnp.where(place == 0, 0.0, pltpu.roll(field, 1, 0))
        right = jnp.where(place == width - 1, 0.0, pltpu.roll(field, size - 1, 0))
        return left.astype(low), field.astype(low), right.astype(low)

    def combine(three, pair_weights, edge_weights, contract):
        left, middle, right = three
        a = dot(jnp.concatenate([left, middle], axis=1), pair_weights, contract)
        b = dot(jnp.concatenate([down(right), right], axis=1), edge_weights, contract)
        c = channels
        return a[:, c : 2 * c] + b[:, :c] + down(a[:, :c]) + up(a[:, 2 * c :] + b[:, c:])

    def conv(n, field):
        return combine(sides(field), ahead_pair[n], ahead_edge[n], NN)

    def apply_map(field, slot):
        return field + dot(field.astype(low), maps[slot].astype(low))

    def apply_flipped(field, slot):
        return field + dot(field.astype(low), maps[slot].astype(low), NT)

    def split(field):
        return tuple(field[at : at + area] for at in range(0, field.shape[0], area))

    def join(fields):
        return jnp.concatenate(fields, axis=0)

    def span(i):
        return slice(i * area, (i + 1) * area)

    def advance(n, states):
        return tuple(
            state + step_size * jnp.tanh(conv(n, state) + biases[pl.ds(n, 1), :]) for state in states
        )

    def trajectory(part, state):
        def step(n, states):
            after = []
            for i, state in enumerate(states):
                states_low[n, part, span(i)] = state.astype(low)
                activation = jnp.tanh(conv(n, state) + biases[pl.ds(n, 1), :])
                slopes[n, part, span(i)] = activation
                after.append(state + step_size * activation)
            return tuple(after)

        return join(lax.fori_loop(0, blocks, step, split(state), unroll=4))

    def change_of(n, part, adjoint, i):
        slope = slopes[n, part, span(i)]
        return step_size * (1.0 - slope * slope) * adjoint

    def retreat(part, adjoint):
        def step(i, adjoints):
            n = blocks - 1 - i
            return tuple(
                adjoint + combine(sides(change_of(n, part, adjoint, at)), back_pair[n], back_edge[n], NT)
                for at, adjoint in enumerate(adjoints)
            )

        return join(lax.fori_loop(0, blocks, step, split(adjoint), unroll=4))

    divisor = 1.0 / images_all

    def sweep(part, adjoint, first=0):
        def step(i, adjoints):
            n = blocks - 1 - i
            after = []
            spots = []
            for at, adjoint in enumerate(adjoints):
                change = change_of(n, part, adjoint, first + at)
                bg_out[pl.ds(n, 1), :] += jnp.sum(change, axis=0, keepdims=True) * divisor
                three = sides(change)
                after.append(adjoint + combine(three, back_pair[n], back_edge[n], NT))
                line = jnp.concatenate(three, axis=1)
                spots.append(jnp.concatenate([down(line), line, up(line)], axis=1))
            used = states_low[n, part, first * area : (first + len(spots)) * area]
            grads = dot(used, join(spots), TN) * divisor
            for tap in range(9):
                wg_out[n, (8 - tap) * channels : (9 - tap) * channels, :] += grads[
                    :, tap * channels : (tap + 1) * channels
                ]
            return tuple(after)

        return join(lax.fori_loop(0, blocks, step, split(adjoint), unroll=4))

    def out_copy(phase, source, to):
        return pltpu.make_async_remote_copy(
            src_ref=residue.at[phase, rows_of(to)],
            dst_ref=gathered.at[phase, source],
            send_sem=out_send.at[phase, to],
            recv_sem=out_recv.at[phase, source],
            device_id={"layer": to},
            device_id_type=MESH,
        )

    def back_copy(phase, source, to):
        return pltpu.make_async_remote_copy(
            src_ref=spread.at[phase, to],
            dst_ref=error.at[phase, rows_of(source)],
            send_sem=back_send.at[phase, to],
            recv_sem=back_recv.at[phase, source],
            device_id={"layer": to},
            device_id_type=MESH,
        )

    def chain_start(phase, value):
        residue[phase] = value
        others(lambda ahead, to: out_copy(phase, me, to).start())
        gathered[phase, me] = residue[phase, rows_of(me)]

    def chain_scan(phase):
        def step(i, carried):
            k = i if phase == 0 else groups - 1 - i

            @pl.when(k != me)
            def _():
                spread[phase, k] = carried
                back_copy(phase, me, k).start()
                out_copy(phase, k, me).wait_recv()

            @pl.when(k == me)
            def _():
                error[phase, rows_of(me)] = carried

            mapped = apply_map(carried, k) if phase == 0 else apply_flipped(carried, k)
            return mapped + gathered[phase, k]

        lax.fori_loop(0, groups, step, jnp.zeros((share, channels), jnp.float32))

    def chain_finish(phase):
        others(lambda ahead, to: back_copy(phase, to, me).wait_recv())
        return error[phase]


    def nth_other(i):
        back_side = parts - 1 - z
        paired = jnp.where(z < back_side, z, back_side)
        near = i // 2 + 1
        outward = jnp.where(z > back_side, near, -near)
        near_part = jnp.where(i % 2 == 0, z + outward, z - outward)
        far = i - paired + 1
        far_part = jnp.where(z > back_side, z - far, z + far)
        return jnp.where(i < 2 * paired, near_part, far_part)

    def start_of(field):
        return jnp.where(me == 0, field, apply_map(field, jnp.where(me == 0, me, before)))

    def relax(start):
        return join(lax.fori_loop(0, blocks, advance, split(start), unroll=4))

    def relax_other(i):
        @pl.when(lead)
        def _():
            part = nth_other(i)
            start = start_of(part_images[part])
            other_starts[part] = start
            other_fine[part] = relax(start)

    def share_on(i):
        part = nth_other(i)
        share_copy(part, z).wait_recv()
        odd_others(lambda to: spread_copy(part, me, to).start())

    def retreat_other(i):
        @pl.when(jnp.logical_not(lead))
        def _():
            part = nth_other(i)
            others(lambda ahead, source: spread_copy(part, source, me).wait_recv())
            ends = ends_of(part_grads[part])
            other_starts[part] = ends
            other_fine[part] = retreat(part, ends)

    def pass_copy(which, part, i):
        where = pl.ds(i * piece, piece)
        return pltpu.make_async_remote_copy(
            src_ref=handoff.at[part, where],
            dst_ref=line[which].at[part, where],
            send_sem=pass_send.at[part, i],
            recv_sem=pass_recv.at[which, part, i],
            device_id={"layer": partner},
            device_id_type=MESH,
        )

    def pass_on(which, i, pieces=range(count)):
        part = nth_other(i)
        apply = apply_map if which == 0 else apply_flipped

        @pl.when(takes(which))
        def _():
            for at in pieces:
                where = slice(at * piece, (at + 1) * piece)
                change = line[which][part, where] - other_starts[part, where]
                handoff[part, where] = apply(change, me) + other_fine[part, where]
                pass_copy(which, part, at).start()

    def pass_wait(which, i, pieces=range(count)):
        part = nth_other(i)

        @pl.when(jnp.logical_not(takes(which)))
        def _():
            for at in pieces:
                pass_copy(which, part, at).wait_recv()

    def other_trajectory(i):
        part = nth_other(i)
        trajectory(part, states_all[part])

    start_image = part_images[z]

    @pl.when(me != 0)
    def _():
        map_copy(before, me).wait_recv()

    starts = start_of(start_image)
    chain_start(0, relax(starts) - apply_map(start_image, me))

    same_side(hand_on)

    def wait_map(ahead, source):
        @pl.when((lax.rem(source - me + groups, pair) != 0) & ((source != before) | (me == 0)))
        def _():
            map_copy(source, me).wait_recv()

    if pair == 2:
        others(wait_map)
    def ends_of(field):
        return jnp.where(me == last, field, apply_flipped(field, after))

    end = end_grad[...]
    ends_adj = ends_of(end)
    back = apply_flipped(end, me)
    others_count = parts - 1

    def images_on(i):
        if i < others_count:
            line_round(2, i + 1)

    def relax_on(i):
        if i < others_count:
            relax_other(i)

    def states_on(i):
        if i < others_count:
            line_round(0, i + 1)
            pass_on(0, i)

    def follow(i):
        if i < others_count:
            pass_wait(0, i)
            other_trajectory(i)
            retreat_other(i)

    chain_scan(0)
    for i in range(others_count):
        share_on(i)
    images_on(0)
    relax_on(0)
    corrected = starts + chain_finish(0)
    states_all[z] = corrected
    line_start(0)
    both_out[0] = trajectory(z, corrected)

    chain_start(1, retreat(z, ends_adj) - back)
    images_on(1)
    relax_on(1)
    states_on(0)
    follow(0)
    chain_scan(1)
    images_on(2)
    relax_on(2)
    states_on(1)
    follow(1)
    adjoint = ends_adj + chain_finish(1)
    adj_all[z] = adjoint
    line_start(1)
    for i in range(2, others_count):
        if i > 2:
            images_on(i)
            relax_on(i)
        states_on(i)
    both_out[1] = sweep(z, adjoint)
    for i in range(2, others_count):
        follow(i)
    for i in range(others_count - 1):
        line_round(1, i + 1)
        pass_on(1, i)
        pass_wait(1, i)
        part = nth_other(i)
        sweep(part, adj_all[part])
    if parts > 1:
        part = nth_other(parts - 2)
        for i in range(count):
            line_round(1, parts - 1, (i,))
            pass_on(1, parts - 2, (i,))
            pass_wait(1, parts - 2, (i,))
            sweep(part, adj_all[part, i * piece : (i + 1) * piece], i)

    def map_sent(to):
        if pair == 1:

            @pl.when(to != after)
            def _():
                map_copy(me, to).wait_send()

        else:
            map_copy(me, to).wait_send()

            @pl.when(is_handed(to))
            def _():
                hand_copy(to).wait_send()

    map_copy(me, after).wait_send()
    if pair == 2:

        @pl.when(partner != after)
        def _():
            map_copy(me, partner).wait_send()

    same_side(map_sent)

    def sent(ahead, to):
        for phase in range(2):
            out_copy(phase, me, to).wait_send()
            back_copy(phase, me, to).wait_send()

    others(sent)
    for which in range(3):
        for away in range(parts):

            @pl.when(takes(which) & (z - away >= 0) & not_last)
            def _():
                for part in range(count):
                    line_copy(which, z - away, part, z + 1, right_send).wait_send()

            @pl.when(takes(which) & (z + away < parts) & not_first)
            def _():
                for part in range(count):
                    line_copy(which, z + away, part, z - 1, left_send).wait_send()

    other_planes(lambda to: share_copy(z, to).wait_send(), me >= 0)

    def passed(part):
        for i in range(count):
            for which in range(2):

                @pl.when(takes(which))
                def _():
                    pass_copy(which, part, i).wait_send()

        odd_others(lambda to: spread_copy(part, me, to).wait_send())

    other_planes(passed, me >= 0)


def shards(images, weights, biases, end_grad):
    groups = lax.axis_size("layer")
    parts = lax.axis_size("dp")
    count, height, width, channels = images.shape
    blocks = weights.shape[0]
    rows = count * height * width
    dims = (groups, parts, count, height, width, count * parts)
    f32 = jnp.float32
    share = rows // groups
    dma = pltpu.SemaphoreType.DMA
    vmem = pl.BlockSpec(memory_space=pltpu.VMEM)
    both, wg, bg = pl.pallas_call(
        functools.partial(kernel, dims),
        out_shape=(
            pltpu.VMEM((2, rows, channels), f32),
            pltpu.VMEM((blocks, 9 * channels, channels), f32),
            pltpu.VMEM((blocks, channels), f32),
        ),
        in_specs=[pl.BlockSpec(memory_space=pltpu.HBM)] * 4,
        out_specs=(vmem,) * 3,
        scratch_shapes=[
            pltpu.VMEM((blocks, 9 * channels, channels), low),
            pltpu.VMEM((blocks, channels), f32),
            pltpu.VMEM((rows, channels), f32),
            dma((4,)),
            pltpu.VMEM((blocks, 2 * channels, 3 * channels), low),
            pltpu.VMEM((blocks, 2 * channels, 2 * channels), low),
            pltpu.VMEM((blocks, 3 * channels, 2 * channels), low),
            pltpu.VMEM((blocks, 2 * channels, 2 * channels), low),
            pltpu.VMEM((groups, channels, channels), f32),
            pltpu.VMEM((blocks, parts, rows, channels), low),
            pltpu.VMEM((blocks, parts, rows, channels), f32),
            pltpu.VMEM((parts, rows, channels), f32),
            pltpu.VMEM((parts, rows, channels), f32),
            pltpu.VMEM((2, rows, channels), f32),
            pltpu.VMEM((2, groups, share, channels), f32),
            pltpu.VMEM((2, groups, share, channels), f32),
            pltpu.VMEM((2, rows, channels), f32),
            dma((groups,)),
            dma((groups,)),
            dma((groups,)),
            dma((2, groups)),
            dma((2, groups)),
            dma((2, groups)),
            dma((2, groups)),
            dma((3, parts, count)),
            dma((3, parts, count)),
            dma((3, parts, count)),
            pltpu.VMEM((parts, rows, channels), f32),
            pltpu.VMEM((parts, rows, channels), f32),
            pltpu.VMEM((parts, rows, channels), f32),
            pltpu.VMEM((parts, rows, channels), f32),
            dma((parts, count)),
            dma((2, parts, count)),
            pltpu.VMEM((parts, rows, channels), f32),
            dma((parts,)),
            dma((parts,)),
            dma((parts, groups // 2)),
            dma((parts, groups)),
        ],
        compiler_params=pltpu.CompilerParams(
            collective_id=0, has_side_effects=True, vmem_limit_bytes=61 << 20
        ),
    )(
        images.reshape(rows, channels),
        weights.reshape(blocks, 9 * channels, channels),
        biases,
        end_grad.reshape(rows, channels),
    )
    shape = (1,) + images.shape
    return (both[0].reshape(shape), both[1].reshape(shape), wg.reshape(weights.shape), bg)


def solution(mesh):
    in_specs = (
        P("dp", None, None, None),
        P("layer", None, None, None, None),
        P("layer", None),
        P("dp", None, None, None),
    )
    out_specs = (
        P("layer", "dp", None, None, None),
        P("layer", "dp", None, None, None),
        P("layer", None, None, None, None),
        P("layer", None),
    )
    return jax.shard_map(shards, mesh=mesh, in_specs=in_specs, out_specs=out_specs, check_vma=False)
```

```python
import functools

import jax
import jax.numpy as jnp
from jax import lax
from jax.experimental import pallas as pl
from jax.experimental.pallas import tpu as pltpu
from jax.sharding import PartitionSpec as P

step_size = 0.25
MESH = pl.DeviceIdType.MESH
low = jnp.bfloat16


def dot(a, b, contract=((1,), (0,))):
    return lax.dot_general(a, b, (contract, ((), ())), preferred_element_type=jnp.float32)


NN = ((1,), (0,))
NT = ((1,), (1,))
TN = ((0,), (0,))


def kernel(
    dims,
    images_in,
    weights_in,
    biases_in,
    end_grad_in,
    both_out,
    wg_out,
    bg_out,
    weights,
    biases,
    end_grad,
    load_sems,
    ahead_pair,
    ahead_edge,
    back_pair,
    back_edge,
    maps,
    states_low,
    slopes,
    states_all,
    adj_all,
    residue,
    gathered,
    spread,
    error,
    map_send,
    map_recv,
    hand_send,
    out_send,
    out_recv,
    back_send,
    back_recv,
    right_send,
    left_send,
    line_recv,
    part_images,
    other_starts,
    other_fine,
    handoff,
    pass_send,
    pass_recv,
    part_grads,
    share_send,
    share_recv,
    spread_send,
    spread_recv,
):
    groups, parts, count, height, width, images_all = dims
    rows, channels = images_in.shape
    blocks = weights_in.shape[0]
    share = rows // groups
    me = lax.axis_index("layer")
    z = lax.axis_index("dp")
    not_first = z > 0
    not_last = z < parts - 1

    def others(body):
        def step(ahead, _):
            body(ahead, lax.rem(me + ahead, groups))
            return 0

        lax.fori_loop(1, groups, step, 0)

    loads = [
        pltpu.make_async_copy(source, target, load_sems.at[i])
        for i, (source, target) in enumerate(
            ((weights_in, weights), (images_in, part_images.at[z]), (biases_in, biases), (end_grad_in, end_grad))
        )
    ]
    for load in loads:
        load.start()
    barrier = pltpu.get_barrier_semaphore()
    others(lambda ahead, to: pl.semaphore_signal(barrier, inc=1, device_id={"layer": to}, device_id_type=MESH))

    for ahead in range(1, parts):
        pl.semaphore_signal(
            barrier, inc=1, device_id={"dp": lax.rem(z + ahead, parts)}, device_id_type=MESH
        )

    loads[0].wait()
    centre = slice(4 * channels, 5 * channels)
    total = weights[0, centre, :].astype(jnp.float32)
    for n in range(1, blocks):
        total = total + weights[n, centre, :].astype(jnp.float32)
    maps[me] = step_size * total

    pl.semaphore_wait(barrier, groups - 1 + parts - 1)

    def map_copy(slot, to):
        return pltpu.make_async_remote_copy(
            src_ref=maps.at[slot],
            dst_ref=maps.at[slot],
            send_sem=map_send.at[to],
            recv_sem=map_recv.at[slot],
            device_id={"layer": to},
            device_id_type=MESH,
        )

    last = groups - 1
    after = lax.rem(me + 1, groups)
    before = lax.rem(me + last, groups)
    pair = 2 if groups % 2 == 0 else 1
    partner = me + 1 - 2 * lax.rem(me, 2) if pair == 2 else me

    def same_side(body):
        def step(ahead, _):
            body(lax.rem(me + pair * ahead, groups))
            return 0

        lax.fori_loop(1, groups // pair, step, 0)

    map_copy(me, after).start()
    if pair == 2:

        @pl.when(partner != after)
        def _():
            map_copy(me, partner).start()

    def send_map(to):
        if pair == 1:

            @pl.when(to != after)
            def _():
                map_copy(me, to).start()

        else:
            map_copy(me, to).start()

    same_side(send_map)

    def hand_copy(slot):
        return pltpu.make_async_remote_copy(
            src_ref=maps.at[slot],
            dst_ref=maps.at[slot],
            send_sem=hand_send.at[slot],
            recv_sem=map_recv.at[slot],
            device_id={"layer": partner},
            device_id_type=MESH,
        )

    def is_handed(slot):
        return lax.rem(slot + 1, groups) != partner

    def hand_on(slot):
        @pl.when((slot != before) | (me == 0))
        def _():
            map_copy(slot, me).wait_recv()

        if pair == 2:

            @pl.when(is_handed(slot))
            def _():
                hand_copy(slot).start()

    for load in loads[1:]:
        load.wait()

    lead = lax.rem(me, 2) == 0

    def rows_of(slot):
        return pl.ds(pl.multiple_of(slot * share, share), share)

    def other_planes(body, who=True):
        for away in range(1, parts):

            @pl.when(who & (z + away < parts))
            def _():
                body(z + away)

            @pl.when(who & (z - away >= 0))
            def _():
                body(z - away)

    def share_copy(part, to):
        return pltpu.make_async_remote_copy(
            src_ref=end_grad.at[rows_of(me)],
            dst_ref=part_grads.at[part, rows_of(me)],
            send_sem=share_send.at[to],
            recv_sem=share_recv.at[part],
            device_id={"dp": to},
            device_id_type=MESH,
        )

    def spread_copy(part, source, to):
        return pltpu.make_async_remote_copy(
            src_ref=part_grads.at[part, rows_of(source)],
            dst_ref=part_grads.at[part, rows_of(source)],
            send_sem=spread_send.at[part, to // 2],
            recv_sem=spread_recv.at[part, source],
            device_id={"layer": to},
            device_id_type=MESH,
        )

    def odd_others(body):
        def step(i, _):
            to = 2 * i + 1

            @pl.when(to != me)
            def _():
                body(to)

            return 0

        lax.fori_loop(0, groups // 2, step, 0)

    other_planes(lambda to: share_copy(z, to).start(), me >= 0)

    line = (states_all, adj_all, part_images)
    piece = rows // count

    def line_copy(which, block, part, to, sends):
        where = line[which].at[block, part * piece : (part + 1) * piece]
        return pltpu.make_async_remote_copy(
            src_ref=where,
            dst_ref=where,
            send_sem=sends.at[which, block, part],
            recv_sem=line_recv.at[which, block, part],
            device_id={"dp": to},
            device_id_type=MESH,
        )

    def go_right(which, block, part):
        @pl.when(not_last)
        def _():
            line_copy(which, block, part, z + 1, right_send).start()

    def go_left(which, block, part):
        @pl.when(not_first)
        def _():
            line_copy(which, block, part, z - 1, left_send).start()

    def takes(which):
        return jnp.logical_not(lead) if which == 1 else lead

    def line_start(which):
        @pl.when(takes(which))
        def _():
            for part in range(count):
                go_right(which, z, part)
                go_left(which, z, part)

    def line_round(which, away, pieces=range(count)):
        for part in pieces:

            @pl.when(takes(which) & (z - away >= 0))
            def _():
                line_copy(which, z - away, part, z, right_send).wait_recv()
                go_right(which, z - away, part)

            @pl.when(takes(which) & (z + away < parts))
            def _():
                line_copy(which, z + away, part, z, left_send).wait_recv()
                go_left(which, z + away, part)

    line_start(2)

    def prepare(n, _):
        def tap(i, j):
            at = (3 * i + j) * channels
            return weights[n, at : at + channels, :]

        def spot(i):
            return slice(i * channels, (i + 1) * channels)

        nothing = jnp.zeros((channels, channels), low)
        for i in range(3):
            for j in range(2):
                ahead_pair[n, spot(j), spot(i)] = tap(i, j)
                back_pair[n, spot(i), spot(j)] = tap(2 - i, 2 - j)
        ahead_edge[n, spot(0), spot(0)] = tap(0, 2)
        ahead_edge[n, spot(0), spot(1)] = nothing
        ahead_edge[n, spot(1), spot(0)] = tap(1, 2)
        ahead_edge[n, spot(1), spot(1)] = tap(2, 2)
        back_edge[n, spot(0), spot(0)] = tap(2, 0)
        back_edge[n, spot(1), spot(0)] = nothing
        back_edge[n, spot(0), spot(1)] = tap(1, 0)
        back_edge[n, spot(1), spot(1)] = tap(0, 0)
        wg_out[n] = jnp.zeros(wg_out.shape[1:], jnp.float32)
        return 0

    lax.fori_loop(0, blocks, prepare, 0)
    bg_out[...] = jnp.zeros(bg_out.shape, jnp.float32)

    column = lax.rem(lax.broadcasted_iota(jnp.int32, (rows, channels), 0), width)

    area = height * width

    def down(field):
        blank = jnp.zeros((width, field.shape[1]), field.dtype)
        lines = []
        for at in range(0, field.shape[0], area):
            lines += [blank, field[at : at + area - width]]
        return jnp.concatenate(lines, axis=0)

    def up(field):
        blank = jnp.zeros((width, field.shape[1]), field.dtype)
        lines = []
        for at in range(0, field.shape[0], area):
            lines += [field[at + width : at + area], blank]
        return jnp.concatenate(lines, axis=0)

    def sides(field):
        size = field.shape[0]
        place = column[:size]
        left = jnp.where(place == 0, 0.0, pltpu.roll(field, 1, 0))
        right = jnp.where(place == width - 1, 0.0, pltpu.roll(field, size - 1, 0))
        return left.astype(low), field.astype(low), right.astype(low)

    def combine(three, pair_weights, edge_weights, contract):
        left, middle, right = three
        a = dot(jnp.concatenate([left, middle], axis=1), pair_weights, contract)
        b = dot(jnp.concatenate([down(right), right], axis=1), edge_weights, contract)
        c = channels
        return a[:, c : 2 * c] + b[:, :c] + down(a[:, :c]) + up(a[:, 2 * c :] + b[:, c:])

    def conv(n, field):
        return combine(sides(field), ahead_pair[n], ahead_edge[n], NN)

    def apply_map(field, slot):
        return field + dot(field.astype(low), maps[slot].astype(low))

    def apply_flipped(field, slot):
        return field + dot(field.astype(low), maps[slot].astype(low), NT)

    def split(field):
        return tuple(field[at : at + area] for at in range(0, field.shape[0], area))

    def join(fields):
        return jnp.concatenate(fields, axis=0)

    def span(i):
        return slice(i * area, (i + 1) * area)

    def advance(n, states):
        return tuple(
            state + step_size * jnp.tanh(conv(n, state) + biases[pl.ds(n, 1), :]) for state in states
        )

    def trajectory(part, state):
        def step(n, states):
            after = []
            for i, state in enumerate(states):
                states_low[n, part, span(i)] = state.astype(low)
                activation = jnp.tanh(conv(n, state) + biases[pl.ds(n, 1), :])
                slopes[n, part, span(i)] = activation
                after.append(state + step_size * activation)
            return tuple(after)

        return join(lax.fori_loop(0, blocks, step, split(state), unroll=4))

    def change_of(n, part, adjoint, i):
        slope = slopes[n, part, span(i)]
        return step_size * (1.0 - slope * slope) * adjoint

    def retreat(part, adjoint):
        def step(i, adjoints):
            n = blocks - 1 - i
            return tuple(
                adjoint + combine(sides(change_of(n, part, adjoint, at)), back_pair[n], back_edge[n], NT)
                for at, adjoint in enumerate(adjoints)
            )

        return join(lax.fori_loop(0, blocks, step, split(adjoint), unroll=4))

    divisor = 1.0 / images_all

    def sweep(part, adjoint, first=0):
        def step(i, adjoints):
            n = blocks - 1 - i
            after = []
            spots = []
            for at, adjoint in enumerate(adjoints):
                change = change_of(n, part, adjoint, first + at)
                bg_out[pl.ds(n, 1), :] += jnp.sum(change, axis=0, keepdims=True) * divisor
                three = sides(change)
                after.append(adjoint + combine(three, back_pair[n], back_edge[n], NT))
                line = jnp.concatenate(three, axis=1)
                spots.append(jnp.concatenate([down(line), line, up(line)], axis=1))
            used = states_low[n, part, first * area : (first + len(spots)) * area]
            grads = dot(used, join(spots), TN) * divisor
            for tap in range(9):
                wg_out[n, (8 - tap) * channels : (9 - tap) * channels, :] += grads[
                    :, tap * channels : (tap + 1) * channels
                ]
            return tuple(after)

        return join(lax.fori_loop(0, blocks, step, split(adjoint), unroll=4))

    def out_copy(phase, source, to):
        return pltpu.make_async_remote_copy(
            src_ref=residue.at[phase, rows_of(to)],
            dst_ref=gathered.at[phase, source],
            send_sem=out_send.at[phase, to],
            recv_sem=out_recv.at[phase, source],
            device_id={"layer": to},
            device_id_type=MESH,
        )

    def back_copy(phase, source, to):
        return pltpu.make_async_remote_copy(
            src_ref=spread.at[phase, to],
            dst_ref=error.at[phase, rows_of(source)],
            send_sem=back_send.at[phase, to],
            recv_sem=back_recv.at[phase, source],
            device_id={"layer": to},
            device_id_type=MESH,
        )

    def chain_start(phase, value):
        residue[phase] = value
        others(lambda ahead, to: out_copy(phase, me, to).start())
        gathered[phase, me] = residue[phase, rows_of(me)]

    def chain_scan(phase):
        def step(i, carried):
            k = i if phase == 0 else groups - 1 - i

            @pl.when(k != me)
            def _():
                spread[phase, k] = carried
                back_copy(phase, me, k).start()
                out_copy(phase, k, me).wait_recv()

            @pl.when(k == me)
            def _():
                error[phase, rows_of(me)] = carried

            mapped = apply_map(carried, k) if phase == 0 else apply_flipped(carried, k)
            return mapped + gathered[phase, k]

        lax.fori_loop(0, groups, step, jnp.zeros((share, channels), jnp.float32))

    def chain_finish(phase):
        others(lambda ahead, to: back_copy(phase, to, me).wait_recv())
        return error[phase]


    def nth_other(i):
        back_side = parts - 1 - z
        paired = jnp.where(z < back_side, z, back_side)
        near = i // 2 + 1
        outward = jnp.where(z > back_side, near, -near)
        near_part = jnp.where(i % 2 == 0, z + outward, z - outward)
        far = i - paired + 1
        far_part = jnp.where(z > back_side, z - far, z + far)
        return jnp.where(i < 2 * paired, near_part, far_part)

    def start_of(field):
        return jnp.where(me == 0, field, apply_map(field, jnp.where(me == 0, me, before)))

    def relax(start):
        return join(lax.fori_loop(0, blocks, advance, split(start), unroll=4))

    def relax_other(i):
        @pl.when(lead)
        def _():
            part = nth_other(i)
            start = start_of(part_images[part])
            other_starts[part] = start
            other_fine[part] = relax(start)

    def share_on(i):
        part = nth_other(i)
        share_copy(part, z).wait_recv()
        odd_others(lambda to: spread_copy(part, me, to).start())

    def retreat_other(i):
        @pl.when(jnp.logical_not(lead))
        def _():
            part = nth_other(i)
            others(lambda ahead, source: spread_copy(part, source, me).wait_recv())
            ends = ends_of(part_grads[part])
            other_starts[part] = ends
            other_fine[part] = retreat(part, ends)

    def pass_copy(which, part, i):
        where = pl.ds(i * piece, piece)
        return pltpu.make_async_remote_copy(
            src_ref=handoff.at[part, where],
            dst_ref=line[which].at[part, where],
            send_sem=pass_send.at[part, i],
            recv_sem=pass_recv.at[which, part, i],
            device_id={"layer": partner},
            device_id_type=MESH,
        )

    def pass_on(which, i, pieces=range(count)):
        part = nth_other(i)
        apply = apply_map if which == 0 else apply_flipped

        @pl.when(takes(which))
        def _():
            for at in pieces:
                where = slice(at * piece, (at + 1) * piece)
                change = line[which][part, where] - other_starts[part, where]
                handoff[part, where] = apply(change, me) + other_fine[part, where]
                pass_copy(which, part, at).start()

    def pass_wait(which, i, pieces=range(count)):
        part = nth_other(i)

        @pl.when(jnp.logical_not(takes(which)))
        def _():
            for at in pieces:
                pass_copy(which, part, at).wait_recv()

    def other_trajectory(i):
        part = nth_other(i)
        trajectory(part, states_all[part])

    start_image = part_images[z]

    @pl.when(me != 0)
    def _():
        map_copy(before, me).wait_recv()

    starts = start_of(start_image)
    chain_start(0, relax(starts) - apply_map(start_image, me))

    same_side(hand_on)

    def wait_map(ahead, source):
        @pl.when((lax.rem(source - me + groups, pair) != 0) & ((source != before) | (me == 0)))
        def _():
            map_copy(source, me).wait_recv()

    if pair == 2:
        others(wait_map)
    def ends_of(field):
        return jnp.where(me == last, field, apply_flipped(field, after))

    end = end_grad[...]
    ends_adj = ends_of(end)
    back = apply_flipped(end, me)
    others_count = parts - 1

    def images_on(i):
        if i < others_count:
            line_round(2, i + 1)

    def relax_on(i):
        if i < others_count:
            relax_other(i)

    def states_on(i):
        if i < others_count:
            line_round(0, i + 1)
            pass_on(0, i)

    def follow(i):
        if i < others_count:
            pass_wait(0, i)
            other_trajectory(i)

    def answer(i):
        if i < others_count:
            retreat_other(i)

    chain_scan(0)
    for i in range(others_count):
        share_on(i)
    images_on(0)
    relax_on(0)
    corrected = starts + chain_finish(0)
    states_all[z] = corrected
    line_start(0)
    both_out[0] = trajectory(z, corrected)

    chain_start(1, retreat(z, ends_adj) - back)
    images_on(1)
    relax_on(1)
    states_on(0)
    follow(0)
    chain_scan(1)
    answer(0)
    images_on(2)
    relax_on(2)
    states_on(1)
    follow(1)
    answer(1)
    adjoint = ends_adj + chain_finish(1)
    adj_all[z] = adjoint
    line_start(1)
    for i in range(2, others_count):
        if i > 2:
            images_on(i)
            relax_on(i)
        states_on(i)
    both_out[1] = sweep(z, adjoint)
    for i in range(2, others_count):
        follow(i)
    early = range(count // 2)
    late = range(count // 2, count)
    if parts > 1:
        line_round(1, 1, early)
    for i in range(2, others_count):
        answer(i)
    for i in range(others_count):
        pass_on(1, i, early)
        line_round(1, i + 1, late)
        pass_on(1, i, late)
        if i < others_count - 1:
            pass_wait(1, i)
            part = nth_other(i)
            sweep(part, adj_all[part])
            line_round(1, i + 2, early)
        else:
            part = nth_other(i)
            for at in range(count):
                pass_wait(1, i, (at,))
                sweep(part, adj_all[part, at * piece : (at + 1) * piece], at)

    def map_sent(to):
        if pair == 1:

            @pl.when(to != after)
            def _():
                map_copy(me, to).wait_send()

        else:
            map_copy(me, to).wait_send()

            @pl.when(is_handed(to))
            def _():
                hand_copy(to).wait_send()

    map_copy(me, after).wait_send()
    if pair == 2:

        @pl.when(partner != after)
        def _():
            map_copy(me, partner).wait_send()

    same_side(map_sent)

    def sent(ahead, to):
        for phase in range(2):
            out_copy(phase, me, to).wait_send()
            back_copy(phase, me, to).wait_send()

    others(sent)
    for which in range(3):
        for away in range(parts):

            @pl.when(takes(which) & (z - away >= 0) & not_last)
            def _():
                for part in range(count):
                    line_copy(which, z - away, part, z + 1, right_send).wait_send()

            @pl.when(takes(which) & (z + away < parts) & not_first)
            def _():
                for part in range(count):
                    line_copy(which, z + away, part, z - 1, left_send).wait_send()

    other_planes(lambda to: share_copy(z, to).wait_send(), me >= 0)

    def passed(part):
        for i in range(count):
            for which in range(2):

                @pl.when(takes(which))
                def _():
                    pass_copy(which, part, i).wait_send()

        odd_others(lambda to: spread_copy(part, me, to).wait_send())

    other_planes(passed, me >= 0)


def write_out(both, wg, bg, ends_out, starts_out, wg_out, bg_out, sems):
    copies = [
        pltpu.make_async_copy(source, target, sems.at[i])
        for i, (source, target) in enumerate(
            ((wg, wg_out), (both.at[0], ends_out), (both.at[1], starts_out), (bg, bg_out))
        )
    ]
    for copy in copies:
        copy.start()
    for copy in copies:
        copy.wait()


def shards(images, weights, biases, end_grad):
    groups = lax.axis_size("layer")
    parts = lax.axis_size("dp")
    count, height, width, channels = images.shape
    blocks = weights.shape[0]
    rows = count * height * width
    dims = (groups, parts, count, height, width, count * parts)
    f32 = jnp.float32
    share = rows // groups
    dma = pltpu.SemaphoreType.DMA
    vmem = pl.BlockSpec(memory_space=pltpu.VMEM)
    both, wg, bg = pl.pallas_call(
        functools.partial(kernel, dims),
        out_shape=(
            pltpu.VMEM((2, rows, channels), f32),
            pltpu.VMEM((blocks, 9 * channels, channels), f32),
            pltpu.VMEM((blocks, channels), f32),
        ),
        in_specs=[pl.BlockSpec(memory_space=pltpu.HBM)] * 4,
        out_specs=(vmem,) * 3,
        scratch_shapes=[
            pltpu.VMEM((blocks, 9 * channels, channels), low),
            pltpu.VMEM((blocks, channels), f32),
            pltpu.VMEM((rows, channels), f32),
            dma((4,)),
            pltpu.VMEM((blocks, 2 * channels, 3 * channels), low),
            pltpu.VMEM((blocks, 2 * channels, 2 * channels), low),
            pltpu.VMEM((blocks, 3 * channels, 2 * channels), low),
            pltpu.VMEM((blocks, 2 * channels, 2 * channels), low),
            pltpu.VMEM((groups, channels, channels), f32),
            pltpu.VMEM((blocks, parts, rows, channels), low),
            pltpu.VMEM((blocks, parts, rows, channels), f32),
            pltpu.VMEM((parts, rows, channels), f32),
            pltpu.VMEM((parts, rows, channels), f32),
            pltpu.VMEM((2, rows, channels), f32),
            pltpu.VMEM((2, groups, share, channels), f32),
            pltpu.VMEM((2, groups, share, channels), f32),
            pltpu.VMEM((2, rows, channels), f32),
            dma((groups,)),
            dma((groups,)),
            dma((groups,)),
            dma((2, groups)),
            dma((2, groups)),
            dma((2, groups)),
            dma((2, groups)),
            dma((3, parts, count)),
            dma((3, parts, count)),
            dma((3, parts, count)),
            pltpu.VMEM((parts, rows, channels), f32),
            pltpu.VMEM((parts, rows, channels), f32),
            pltpu.VMEM((parts, rows, channels), f32),
            pltpu.VMEM((parts, rows, channels), f32),
            dma((parts, count)),
            dma((2, parts, count)),
            pltpu.VMEM((parts, rows, channels), f32),
            dma((parts,)),
            dma((parts,)),
            dma((parts, groups // 2)),
            dma((parts, groups)),
        ],
        compiler_params=pltpu.CompilerParams(
            collective_id=0, has_side_effects=True, vmem_limit_bytes=61 << 20
        ),
    )(
        images.reshape(rows, channels),
        weights.reshape(blocks, 9 * channels, channels),
        biases,
        end_grad.reshape(rows, channels),
    )
    shape = (1,) + images.shape
    hbm = pl.BlockSpec(memory_space=pltpu.HBM)
    ends, starts, wg, bg = pl.pallas_call(
        write_out,
        out_shape=(
            jax.ShapeDtypeStruct((rows, channels), f32),
            jax.ShapeDtypeStruct((rows, channels), f32),
            jax.ShapeDtypeStruct((blocks, 9 * channels, channels), f32),
            jax.ShapeDtypeStruct((blocks, channels), f32),
        ),
        in_specs=[vmem] * 3,
        out_specs=(hbm,) * 4,
        scratch_shapes=[dma((4,))],
        compiler_params=pltpu.CompilerParams(vmem_limit_bytes=1 << 20),
    )(*(pltpu.with_memory_space_constraint(x, pltpu.VMEM) for x in (both, wg, bg)))
    return (ends.reshape(shape), starts.reshape(shape), wg.reshape(weights.shape), bg)


def solution(mesh):
    in_specs = (
        P("dp", None, None, None),
        P("layer", None, None, None, None),
        P("layer", None),
        P("dp", None, None, None),
    )
    out_specs = (
        P("layer", "dp", None, None, None),
        P("layer", "dp", None, None, None),
        P("layer", None, None, None, None),
        P("layer", None),
    )
    return jax.shard_map(shards, mesh=mesh, in_specs=in_specs, out_specs=out_specs, check_vma=False)
```

```python
import functools

import jax
import jax.numpy as jnp
from jax import lax
from jax.experimental import pallas as pl
from jax.experimental.pallas import tpu as pltpu
from jax.sharding import PartitionSpec as P

step_size = 0.25
MESH = pl.DeviceIdType.MESH
low = jnp.bfloat16


def dot(a, b, contract=((1,), (0,))):
    return lax.dot_general(a, b, (contract, ((), ())), preferred_element_type=jnp.float32)


NN = ((1,), (0,))
NT = ((1,), (1,))
TN = ((0,), (0,))


def kernel(
    dims,
    images_in,
    weights_in,
    biases_in,
    end_grad_in,
    both_out,
    wg_out,
    bg_out,
    weights,
    biases,
    end_grad,
    load_sems,
    ahead_pair,
    ahead_edge,
    back_pair,
    back_edge,
    maps,
    states_low,
    slopes,
    states_all,
    adj_all,
    residue,
    gathered,
    spread,
    error,
    map_send,
    map_recv,
    hand_send,
    out_send,
    out_recv,
    back_send,
    back_recv,
    right_send,
    left_send,
    line_recv,
    part_images,
    other_starts,
    other_fine,
    handoff,
    pass_send,
    pass_recv,
    part_grads,
    share_send,
    share_recv,
    spread_send,
    spread_recv,
    pair_maps,
):
    groups, parts, count, height, width, images_all = dims
    rows, channels = images_in.shape
    blocks = weights_in.shape[0]
    share = rows // groups
    me = lax.axis_index("layer")
    z = lax.axis_index("dp")
    not_first = z > 0
    not_last = z < parts - 1

    def others(body):
        def step(ahead, _):
            body(ahead, lax.rem(me + ahead, groups))
            return 0

        lax.fori_loop(1, groups, step, 0)

    loads = [
        pltpu.make_async_copy(source, target, load_sems.at[i])
        for i, (source, target) in enumerate(
            ((weights_in, weights), (images_in, part_images.at[z]), (biases_in, biases), (end_grad_in, end_grad))
        )
    ]
    for load in loads:
        load.start()
    barrier = pltpu.get_barrier_semaphore()
    others(lambda ahead, to: pl.semaphore_signal(barrier, inc=1, device_id={"layer": to}, device_id_type=MESH))

    for ahead in range(1, parts):
        pl.semaphore_signal(
            barrier, inc=1, device_id={"dp": lax.rem(z + ahead, parts)}, device_id_type=MESH
        )

    loads[0].wait()
    centre = slice(4 * channels, 5 * channels)
    total = weights[0, centre, :].astype(jnp.float32)
    for n in range(1, blocks):
        total = total + weights[n, centre, :].astype(jnp.float32)
    maps[me] = step_size * total

    pl.semaphore_wait(barrier, groups - 1 + parts - 1)

    def map_copy(slot, to):
        return pltpu.make_async_remote_copy(
            src_ref=maps.at[slot],
            dst_ref=maps.at[slot],
            send_sem=map_send.at[to],
            recv_sem=map_recv.at[slot],
            device_id={"layer": to},
            device_id_type=MESH,
        )

    last = groups - 1
    after = jnp.minimum(me + 1, last)
    before = jnp.maximum(me - 1, 0)
    partner = me + 1 - 2 * lax.rem(me, 2)
    inner = (me > 0) & (me < last)

    def same_side(body):
        def step(ahead, _):
            body(lax.rem(me + 2 * ahead, groups))
            return 0

        lax.fori_loop(1, groups // 2, step, 0)

    def map_sends(body):
        @pl.when(me < last)
        def _():
            body(after)

        @pl.when(lax.rem(me, 2) == 1)
        def _():
            body(partner)

        @pl.when(inner)
        def _():
            same_side(body)

    map_sends(lambda to: map_copy(me, to).start())

    def hand_copy(slot):
        return pltpu.make_async_remote_copy(
            src_ref=maps.at[slot],
            dst_ref=maps.at[slot],
            send_sem=hand_send.at[slot],
            recv_sem=map_recv.at[slot],
            device_id={"layer": partner},
            device_id_type=MESH,
        )

    def is_handed(slot):
        return (slot > 0) & (slot < last) & (slot + 1 != partner)

    def hand_on(slot):
        @pl.when((slot > 0) & (slot < last))
        def _():
            map_copy(slot, me).wait_recv()

        @pl.when(is_handed(slot))
        def _():
            hand_copy(slot).start()

    for load in loads[1:]:
        load.wait()

    lead = lax.rem(me, 2) == 0

    def rows_of(slot):
        return pl.ds(pl.multiple_of(slot * share, share), share)

    def other_planes(body, who=True):
        for away in range(1, parts):

            @pl.when(who & (z + away < parts))
            def _():
                body(z + away)

            @pl.when(who & (z - away >= 0))
            def _():
                body(z - away)

    def share_copy(part, to):
        return pltpu.make_async_remote_copy(
            src_ref=end_grad.at[rows_of(me)],
            dst_ref=part_grads.at[part, rows_of(me)],
            send_sem=share_send.at[to],
            recv_sem=share_recv.at[part],
            device_id={"dp": to},
            device_id_type=MESH,
        )

    def spread_copy(part, source, to):
        return pltpu.make_async_remote_copy(
            src_ref=part_grads.at[part, rows_of(source)],
            dst_ref=part_grads.at[part, rows_of(source)],
            send_sem=spread_send.at[part, to // 2],
            recv_sem=spread_recv.at[part, source],
            device_id={"layer": to},
            device_id_type=MESH,
        )

    def odd_others(body):
        def step(i, _):
            to = 2 * i + 1

            @pl.when(to != me)
            def _():
                body(to)

            return 0

        lax.fori_loop(0, groups // 2, step, 0)

    other_planes(lambda to: share_copy(z, to).start(), me >= 0)

    line = (states_all, adj_all, part_images)
    piece = rows // count

    def line_copy(which, block, part, to, sends):
        where = line[which].at[block, part * piece : (part + 1) * piece]
        return pltpu.make_async_remote_copy(
            src_ref=where,
            dst_ref=where,
            send_sem=sends.at[which, block, part],
            recv_sem=line_recv.at[which, block, part],
            device_id={"dp": to},
            device_id_type=MESH,
        )

    def go_right(which, block, part):
        @pl.when(not_last)
        def _():
            line_copy(which, block, part, z + 1, right_send).start()

    def go_left(which, block, part):
        @pl.when(not_first)
        def _():
            line_copy(which, block, part, z - 1, left_send).start()

    def takes(which):
        return jnp.logical_not(lead) if which == 1 else lead

    def line_start(which):
        @pl.when(takes(which))
        def _():
            for part in range(count):
                go_right(which, z, part)
                go_left(which, z, part)

    def line_round(which, away, pieces=range(count)):
        for part in pieces:

            @pl.when(takes(which) & (z - away >= 0))
            def _():
                line_copy(which, z - away, part, z, right_send).wait_recv()
                go_right(which, z - away, part)

            @pl.when(takes(which) & (z + away < parts))
            def _():
                line_copy(which, z + away, part, z, left_send).wait_recv()
                go_left(which, z + away, part)

    line_start(2)

    def prepare(n, _):
        def tap(i, j):
            at = (3 * i + j) * channels
            return weights[n, at : at + channels, :]

        def spot(i):
            return slice(i * channels, (i + 1) * channels)

        nothing = jnp.zeros((channels, channels), low)
        for i in range(3):
            for j in range(2):
                ahead_pair[n, spot(j), spot(i)] = tap(i, j)
                back_pair[n, spot(i), spot(j)] = tap(2 - i, 2 - j)
        ahead_edge[n, spot(0), spot(0)] = tap(0, 2)
        ahead_edge[n, spot(0), spot(1)] = nothing
        ahead_edge[n, spot(1), spot(0)] = tap(1, 2)
        ahead_edge[n, spot(1), spot(1)] = tap(2, 2)
        back_edge[n, spot(0), spot(0)] = tap(2, 0)
        back_edge[n, spot(1), spot(0)] = nothing
        back_edge[n, spot(0), spot(1)] = tap(1, 0)
        back_edge[n, spot(1), spot(1)] = tap(0, 0)
        wg_out[n] = jnp.zeros(wg_out.shape[1:], jnp.float32)
        return 0

    lax.fori_loop(0, blocks, prepare, 0)
    bg_out[...] = jnp.zeros(bg_out.shape, jnp.float32)

    column = lax.rem(lax.broadcasted_iota(jnp.int32, (rows, channels), 0), width)

    area = height * width

    def down(field):
        blank = jnp.zeros((width, field.shape[1]), field.dtype)
        lines = []
        for at in range(0, field.shape[0], area):
            lines += [blank, field[at : at + area - width]]
        return jnp.concatenate(lines, axis=0)

    def up(field):
        blank = jnp.zeros((width, field.shape[1]), field.dtype)
        lines = []
        for at in range(0, field.shape[0], area):
            lines += [field[at + width : at + area], blank]
        return jnp.concatenate(lines, axis=0)

    def sides(field):
        size = field.shape[0]
        place = column[:size]
        left = jnp.where(place == 0, 0.0, pltpu.roll(field, 1, 0))
        right = jnp.where(place == width - 1, 0.0, pltpu.roll(field, size - 1, 0))
        return left.astype(low), field.astype(low), right.astype(low)

    def combine(three, pair_weights, edge_weights, contract):
        left, middle, right = three
        a = dot(jnp.concatenate([left, middle], axis=1), pair_weights, contract)
        b = dot(jnp.concatenate([down(right), right], axis=1), edge_weights, contract)
        c = channels
        return a[:, c : 2 * c] + b[:, :c] + down(a[:, :c]) + up(a[:, 2 * c :] + b[:, c:])

    def conv(n, field):
        return combine(sides(field), ahead_pair[n], ahead_edge[n], NN)

    def apply_map(field, slot, table=maps):
        return field + dot(field.astype(low), table[slot].astype(low))

    def apply_flipped(field, slot, table=maps):
        return field + dot(field.astype(low), table[slot].astype(low), NT)

    def split(field):
        return tuple(field[at : at + area] for at in range(0, field.shape[0], area))

    def join(fields):
        return jnp.concatenate(fields, axis=0)

    def span(i):
        return slice(i * area, (i + 1) * area)

    def advance(n, states):
        return tuple(
            state + step_size * jnp.tanh(conv(n, state) + biases[pl.ds(n, 1), :]) for state in states
        )

    def trajectory(part, state):
        def step(n, states):
            after = []
            for i, state in enumerate(states):
                states_low[n, part, span(i)] = state.astype(low)
                activation = jnp.tanh(conv(n, state) + biases[pl.ds(n, 1), :])
                slopes[n, part, span(i)] = activation
                after.append(state + step_size * activation)
            return tuple(after)

        return join(lax.fori_loop(0, blocks, step, split(state), unroll=4))

    def change_of(n, part, adjoint, i):
        slope = slopes[n, part, span(i)]
        return step_size * (1.0 - slope * slope) * adjoint

    def retreat(part, adjoint):
        def step(i, adjoints):
            n = blocks - 1 - i
            return tuple(
                adjoint + combine(sides(change_of(n, part, adjoint, at)), back_pair[n], back_edge[n], NT)
                for at, adjoint in enumerate(adjoints)
            )

        return join(lax.fori_loop(0, blocks, step, split(adjoint), unroll=4))

    divisor = 1.0 / images_all

    def sweep(part, adjoint, first=0):
        def step(i, adjoints):
            n = blocks - 1 - i
            after = []
            spots = []
            for at, adjoint in enumerate(adjoints):
                change = change_of(n, part, adjoint, first + at)
                bg_out[pl.ds(n, 1), :] += jnp.sum(change, axis=0, keepdims=True) * divisor
                three = sides(change)
                after.append(adjoint + combine(three, back_pair[n], back_edge[n], NT))
                line = jnp.concatenate(three, axis=1)
                spots.append(jnp.concatenate([down(line), line, up(line)], axis=1))
            used = states_low[n, part, first * area : (first + len(spots)) * area]
            grads = dot(used, join(spots), TN) * divisor
            for tap in range(9):
                wg_out[n, (8 - tap) * channels : (9 - tap) * channels, :] += grads[
                    :, tap * channels : (tap + 1) * channels
                ]
            return tuple(after)

        return join(lax.fori_loop(0, blocks, step, split(adjoint), unroll=4))

    def out_copy(phase, source, to):
        return pltpu.make_async_remote_copy(
            src_ref=residue.at[phase, rows_of(to)],
            dst_ref=gathered.at[phase, source],
            send_sem=out_send.at[phase, to],
            recv_sem=out_recv.at[phase, source],
            device_id={"layer": to},
            device_id_type=MESH,
        )

    def back_copy(phase, source, to):
        return pltpu.make_async_remote_copy(
            src_ref=spread.at[phase, to],
            dst_ref=error.at[phase, rows_of(source)],
            send_sem=back_send.at[phase, to],
            recv_sem=back_recv.at[phase, source],
            device_id={"layer": to},
            device_id_type=MESH,
        )

    pairs = groups // 2
    ends = (0, last)

    def chain_start(phase, value):
        residue[phase] = value

        @pl.when(me != ends[1 - phase])
        def _():
            others(lambda ahead, to: out_copy(phase, me, to).start())

        gathered[phase, me] = residue[phase, rows_of(me)]

    def pair_up(m, _):
        one = maps[2 * m]
        two = maps[2 * m + 1]
        pair_maps[m] = one + two + dot(one.astype(low), two.astype(low))
        return 0

    def chain_scan(phase):
        apply = apply_map if phase == 0 else apply_flipped

        def deliver(k, value):
            @pl.when(k != me)
            def _():
                spread[phase, k] = value
                back_copy(phase, me, k).start()

            @pl.when(k == me)
            def _():
                error[phase, rows_of(me)] = value

        def arrived(k):
            @pl.when(k != me)
            def _():
                out_copy(phase, k, me).wait_recv()

        def pair_of(i):
            m = i if phase == 0 else pairs - 1 - i
            return 2 * m + phase, 2 * m + 1 - phase, m

        def step(i, carried):
            one, two, m = pair_of(i)
            deliver(one, carried)
            moved = apply(carried, one)
            jumped = apply(carried, m, pair_maps)
            arrived(one)
            deliver(two, moved + gathered[phase, one])
            jumped = jumped + apply(gathered[phase, one], two)
            arrived(two)
            return jumped + gathered[phase, two]

        one, two, _ = pair_of(0)
        arrived(one)
        deliver(two, gathered[phase, one])
        carried = apply(gathered[phase, one], two)
        arrived(two)
        carried = lax.fori_loop(1, pairs - 1, step, carried + gathered[phase, two])
        one, two, _ = pair_of(pairs - 1)
        deliver(one, carried)
        moved = apply(carried, one)
        arrived(one)
        deliver(two, moved + gathered[phase, one])

    def chain_finish(phase):
        @pl.when(me != ends[phase])
        def _():
            others(lambda ahead, to: back_copy(phase, to, me).wait_recv())

        return jnp.where(me == ends[phase], 0.0, error[phase])

    def nth_other(i):
        back_side = parts - 1 - z
        paired = jnp.where(z < back_side, z, back_side)
        near = i // 2 + 1
        outward = jnp.where(z > back_side, near, -near)
        near_part = jnp.where(i % 2 == 0, z + outward, z - outward)
        far = i - paired + 1
        far_part = jnp.where(z > back_side, z - far, z + far)
        return jnp.where(i < 2 * paired, near_part, far_part)

    def start_of(field):
        return jnp.where(me == 0, field, apply_map(field, jnp.where(me == 0, me, before)))

    def relax(start):
        return join(lax.fori_loop(0, blocks, advance, split(start), unroll=4))

    def relax_other(i):
        @pl.when(lead)
        def _():
            part = nth_other(i)
            start = start_of(part_images[part])
            other_starts[part] = start
            other_fine[part] = relax(start)

    def share_on(i):
        part = nth_other(i)
        share_copy(part, z).wait_recv()
        odd_others(lambda to: spread_copy(part, me, to).start())

    def retreat_other(i):
        @pl.when(jnp.logical_not(lead))
        def _():
            part = nth_other(i)
            others(lambda ahead, source: spread_copy(part, source, me).wait_recv())
            cotangent = ends_of(part_grads[part])
            other_starts[part] = cotangent
            other_fine[part] = retreat(part, cotangent)

    def pass_copy(which, part, i):
        where = pl.ds(i * piece, piece)
        return pltpu.make_async_remote_copy(
            src_ref=handoff.at[part, where],
            dst_ref=line[which].at[part, where],
            send_sem=pass_send.at[part, i],
            recv_sem=pass_recv.at[which, part, i],
            device_id={"layer": partner},
            device_id_type=MESH,
        )

    def pass_on(which, i, pieces=range(count)):
        part = nth_other(i)
        apply = apply_map if which == 0 else apply_flipped

        @pl.when(takes(which))
        def _():
            for at in pieces:
                where = slice(at * piece, (at + 1) * piece)
                change = line[which][part, where] - other_starts[part, where]
                handoff[part, where] = apply(change, me) + other_fine[part, where]
                pass_copy(which, part, at).start()

    def pass_wait(which, i, pieces=range(count)):
        part = nth_other(i)

        @pl.when(jnp.logical_not(takes(which)))
        def _():
            for at in pieces:
                pass_copy(which, part, at).wait_recv()

    def other_trajectory(i):
        part = nth_other(i)
        trajectory(part, states_all[part])

    start_image = part_images[z]

    @pl.when(me != 0)
    def _():
        map_copy(before, me).wait_recv()

    starts = start_of(start_image)
    chain_start(0, relax(starts) - apply_map(start_image, me))

    same_side(hand_on)

    def wait_map(ahead, source):
        across = lax.rem(source - me + groups, 2) != 0
        sent = (source > 0) & ((source < last) | (me == last - 1))

        @pl.when(across & sent & (source != me - 1))
        def _():
            map_copy(source, me).wait_recv()

    others(wait_map)
    lax.fori_loop(1, pairs - 1, pair_up, 0)

    def ends_of(field):
        return jnp.where(me == last, field, apply_flipped(field, after))

    end = end_grad[...]
    ends_adj = ends_of(end)
    back = apply_flipped(end, me)
    others_count = parts - 1

    def images_on(i):
        if i < others_count:
            line_round(2, i + 1)

    def relax_on(i):
        if i < others_count:
            relax_other(i)

    def states_on(i):
        if i < others_count:
            line_round(0, i + 1)
            pass_on(0, i)

    def follow(i):
        if i < others_count:
            pass_wait(0, i)
            other_trajectory(i)

    def answer(i):
        if i < others_count:
            retreat_other(i)

    chain_scan(0)
    for i in range(others_count):
        share_on(i)
    images_on(0)
    relax_on(0)
    corrected = starts + chain_finish(0)
    states_all[z] = corrected
    line_start(0)
    both_out[0] = trajectory(z, corrected)

    chain_start(1, retreat(z, ends_adj) - back)
    images_on(1)
    relax_on(1)
    states_on(0)
    follow(0)
    chain_scan(1)
    answer(0)
    images_on(2)
    relax_on(2)
    states_on(1)
    follow(1)
    answer(1)
    adjoint = ends_adj + chain_finish(1)
    adj_all[z] = adjoint
    line_start(1)
    for i in range(2, others_count):
        if i > 2:
            images_on(i)
            relax_on(i)
        states_on(i)
    both_out[1] = sweep(z, adjoint)
    for i in range(2, others_count):
        follow(i)
    early = range(count // 2)
    late = range(count // 2, count)
    if parts > 1:
        line_round(1, 1, early)
    for i in range(2, others_count):
        answer(i)
    for i in range(others_count):
        pass_on(1, i, early)
        line_round(1, i + 1, late)
        pass_on(1, i, late)
        if i < others_count - 1:
            pass_wait(1, i)
            part = nth_other(i)
            sweep(part, adj_all[part])
            line_round(1, i + 2, early)
        else:
            part = nth_other(i)
            for at in range(count):
                pass_wait(1, i, (at,))
                sweep(part, adj_all[part, at * piece : (at + 1) * piece], at)

    map_sends(lambda to: map_copy(me, to).wait_send())

    def map_handed(slot):
        @pl.when(is_handed(slot))
        def _():
            hand_copy(slot).wait_send()

    same_side(map_handed)

    def sent(ahead, to):
        for phase in range(2):

            @pl.when(me != ends[1 - phase])
            def _():
                out_copy(phase, me, to).wait_send()

            @pl.when(to != ends[phase])
            def _():
                back_copy(phase, me, to).wait_send()

    others(sent)
    for which in range(3):
        for away in range(parts):

            @pl.when(takes(which) & (z - away >= 0) & not_last)
            def _():
                for part in range(count):
                    line_copy(which, z - away, part, z + 1, right_send).wait_send()

            @pl.when(takes(which) & (z + away < parts) & not_first)
            def _():
                for part in range(count):
                    line_copy(which, z + away, part, z - 1, left_send).wait_send()

    other_planes(lambda to: share_copy(z, to).wait_send(), me >= 0)

    def passed(part):
        for i in range(count):
            for which in range(2):

                @pl.when(takes(which))
                def _():
                    pass_copy(which, part, i).wait_send()

        odd_others(lambda to: spread_copy(part, me, to).wait_send())

    other_planes(passed, me >= 0)


def write_out(both, wg, bg, ends_out, starts_out, wg_out, bg_out, sems):
    copies = [
        pltpu.make_async_copy(source, target, sems.at[i])
        for i, (source, target) in enumerate(
            ((wg, wg_out), (both.at[0], ends_out), (both.at[1], starts_out), (bg, bg_out))
        )
    ]
    for copy in copies:
        copy.start()
    for copy in copies:
        copy.wait()


def shards(images, weights, biases, end_grad):
    groups = lax.axis_size("layer")
    parts = lax.axis_size("dp")
    count, height, width, channels = images.shape
    blocks = weights.shape[0]
    rows = count * height * width
    dims = (groups, parts, count, height, width, count * parts)
    f32 = jnp.float32
    share = rows // groups
    dma = pltpu.SemaphoreType.DMA
    vmem = pl.BlockSpec(memory_space=pltpu.VMEM)
    both, wg, bg = pl.pallas_call(
        functools.partial(kernel, dims),
        out_shape=(
            pltpu.VMEM((2, rows, channels), f32),
            pltpu.VMEM((blocks, 9 * channels, channels), f32),
            pltpu.VMEM((blocks, channels), f32),
        ),
        in_specs=[pl.BlockSpec(memory_space=pltpu.HBM)] * 4,
        out_specs=(vmem,) * 3,
        scratch_shapes=[
            pltpu.VMEM((blocks, 9 * channels, channels), low),
            pltpu.VMEM((blocks, channels), f32),
            pltpu.VMEM((rows, channels), f32),
            dma((4,)),
            pltpu.VMEM((blocks, 2 * channels, 3 * channels), low),
            pltpu.VMEM((blocks, 2 * channels, 2 * channels), low),
            pltpu.VMEM((blocks, 3 * channels, 2 * channels), low),
            pltpu.VMEM((blocks, 2 * channels, 2 * channels), low),
            pltpu.VMEM((groups, channels, channels), f32),
            pltpu.VMEM((blocks, parts, rows, channels), low),
            pltpu.VMEM((blocks, parts, rows, channels), f32),
            pltpu.VMEM((parts, rows, channels), f32),
            pltpu.VMEM((parts, rows, channels), f32),
            pltpu.VMEM((2, rows, channels), f32),
            pltpu.VMEM((2, groups, share, channels), f32),
            pltpu.VMEM((2, groups, share, channels), f32),
            pltpu.VMEM((2, rows, channels), f32),
            dma((groups,)),
            dma((groups,)),
            dma((groups,)),
            dma((2, groups)),
            dma((2, groups)),
            dma((2, groups)),
            dma((2, groups)),
            dma((3, parts, count)),
            dma((3, parts, count)),
            dma((3, parts, count)),
            pltpu.VMEM((parts, rows, channels), f32),
            pltpu.VMEM((parts, rows, channels), f32),
            pltpu.VMEM((parts, rows, channels), f32),
            pltpu.VMEM((parts, rows, channels), f32),
            dma((parts, count)),
            dma((2, parts, count)),
            pltpu.VMEM((parts, rows, channels), f32),
            dma((parts,)),
            dma((parts,)),
            dma((parts, groups // 2)),
            dma((parts, groups)),
            pltpu.VMEM((groups // 2, channels, channels), f32),
        ],
        compiler_params=pltpu.CompilerParams(
            collective_id=0, has_side_effects=True, vmem_limit_bytes=61 << 20
        ),
    )(
        images.reshape(rows, channels),
        weights.reshape(blocks, 9 * channels, channels),
        biases,
        end_grad.reshape(rows, channels),
    )
    shape = (1,) + images.shape
    hbm = pl.BlockSpec(memory_space=pltpu.HBM)
    ends, starts, wg, bg = pl.pallas_call(
        write_out,
        out_shape=(
            jax.ShapeDtypeStruct((rows, channels), f32),
            jax.ShapeDtypeStruct((rows, channels), f32),
            jax.ShapeDtypeStruct((blocks, 9 * channels, channels), f32),
            jax.ShapeDtypeStruct((blocks, channels), f32),
        ),
        in_specs=[vmem] * 3,
        out_specs=(hbm,) * 4,
        scratch_shapes=[dma((4,))],
        compiler_params=pltpu.CompilerParams(vmem_limit_bytes=1 << 20),
    )(*(pltpu.with_memory_space_constraint(x, pltpu.VMEM) for x in (both, wg, bg)))
    return (ends.reshape(shape), starts.reshape(shape), wg.reshape(weights.shape), bg)


def solution(mesh):
    in_specs = (
        P("dp", None, None, None),
        P("layer", None, None, None, None),
        P("layer", None),
        P("dp", None, None, None),
    )
    out_specs = (
        P("layer", "dp", None, None, None),
        P("layer", "dp", None, None, None),
        P("layer", None, None, None, None),
        P("layer", None),
    )
    return jax.shard_map(shards, mesh=mesh, in_specs=in_specs, out_specs=out_specs, check_vma=False)
```

```python
import functools

import jax
import jax.numpy as jnp
from jax import lax
from jax.experimental import pallas as pl
from jax.experimental.pallas import tpu as pltpu
from jax.sharding import PartitionSpec as P

step_size = 0.25
MESH = pl.DeviceIdType.MESH
low = jnp.bfloat16


def dot(a, b, contract=((1,), (0,))):
    return lax.dot_general(a, b, (contract, ((), ())), preferred_element_type=jnp.float32)


NN = ((1,), (0,))
NT = ((1,), (1,))
TN = ((0,), (0,))


def kernel(
    dims,
    images_in,
    weights_in,
    biases_in,
    end_grad_in,
    both_out,
    wg_out,
    bg_out,
    weights,
    biases,
    end_grad,
    load_sems,
    ahead_pair,
    ahead_edge,
    back_pair,
    back_edge,
    maps,
    states_low,
    slopes,
    states_all,
    adj_all,
    residue,
    gathered,
    spread,
    error,
    map_send,
    map_recv,
    hand_send,
    out_send,
    out_recv,
    back_send,
    back_recv,
    right_send,
    left_send,
    line_recv,
    part_images,
    other_starts,
    other_fine,
    handoff,
    pass_send,
    pass_recv,
    part_grads,
    share_send,
    share_recv,
    spread_send,
    spread_recv,
    pair_maps,
    pair_send,
    pair_recv,
    raw,
    lent,
    lend_send,
    lend_recv,
):
    groups, parts, count, height, width, images_all = dims
    rows, channels = images_in.shape
    blocks = weights_in.shape[0]
    share = rows // groups
    me = lax.axis_index("layer")
    z = lax.axis_index("dp")
    not_first = z > 0
    not_last = z < parts - 1

    def others(body):
        def step(ahead, _):
            body(ahead, lax.rem(me + ahead, groups))
            return 0

        lax.fori_loop(1, groups, step, 0)

    loads = [
        pltpu.make_async_copy(source, target, load_sems.at[i])
        for i, (source, target) in enumerate(
            ((weights_in, weights), (images_in, part_images.at[z]), (biases_in, biases), (end_grad_in, end_grad))
        )
    ]
    for load in loads:
        load.start()
    barrier = pltpu.get_barrier_semaphore()
    others(lambda ahead, to: pl.semaphore_signal(barrier, inc=1, device_id={"layer": to}, device_id_type=MESH))

    for ahead in range(1, parts):
        pl.semaphore_signal(
            barrier, inc=1, device_id={"dp": lax.rem(z + ahead, parts)}, device_id_type=MESH
        )

    loads[0].wait()
    centre = slice(4 * channels, 5 * channels)
    total = weights[0, centre, :].astype(jnp.float32)
    for n in range(1, blocks):
        total = total + weights[n, centre, :].astype(jnp.float32)
    maps[me] = step_size * total

    pl.semaphore_wait(barrier, groups - 1 + parts - 1)

    def map_copy(slot, to):
        return pltpu.make_async_remote_copy(
            src_ref=maps.at[slot],
            dst_ref=maps.at[slot],
            send_sem=map_send.at[to],
            recv_sem=map_recv.at[slot],
            device_id={"layer": to},
            device_id_type=MESH,
        )

    last = groups - 1
    after = jnp.minimum(me + 1, last)
    before = jnp.maximum(me - 1, 0)
    partner = me + 1 - 2 * lax.rem(me, 2)
    inner = (me > 0) & (me < last)

    def same_side(body):
        def step(ahead, _):
            body(lax.rem(me + 2 * ahead, groups))
            return 0

        lax.fori_loop(1, groups // 2, step, 0)

    odd = lax.rem(me, 2) == 1
    pairs = groups // 2
    mine = me // 2

    def is_inner(m):
        return (m > 0) & (m < pairs - 1)

    def near_maps(body):
        @pl.when(me != partner)
        def _():
            body(partner)

        @pl.when(odd & (me < last))
        def _():
            body(after)

    def far_maps(body):
        @pl.when(jnp.logical_not(odd) & (me > 0))
        def _():
            body(before)

    near_maps(lambda to: map_copy(me, to).start())

    def pair_copy(m, to, sends):
        return pltpu.make_async_remote_copy(
            src_ref=pair_maps.at[m],
            dst_ref=pair_maps.at[m],
            send_sem=sends,
            recv_sem=pair_recv.at[m],
            device_id={"layer": to},
            device_id_type=MESH,
        )

    def pair_sends(body):
        @pl.when(jnp.logical_not(odd) & is_inner(mine))
        def _():
            same_side(lambda to: body(pair_copy(mine, to, pair_send.at[to // 2])))

    def other_pairs(body):
        def step(m, _):
            @pl.when(m != mine)
            def _():
                body(m)

            return 0

        lax.fori_loop(1, pairs - 1, step, 0)

    def hand_pairs():
        @pl.when(jnp.logical_not(odd))
        def _():
            def hand(m):
                pair_copy(m, me, pair_send.at[m]).wait_recv()
                pair_copy(m, partner, hand_send.at[m]).start()

            other_pairs(hand)

        @pl.when(odd)
        def _():
            other_pairs(lambda m: pair_copy(m, me, pair_send.at[m]).wait_recv())

    for load in loads[1:]:
        load.wait()

    lead = lax.rem(me, 2) == 0

    def rows_of(slot):
        return pl.ds(pl.multiple_of(slot * share, share), share)

    def other_planes(body, who=True):
        for away in range(1, parts):

            @pl.when(who & (z + away < parts))
            def _():
                body(z + away)

            @pl.when(who & (z - away >= 0))
            def _():
                body(z - away)

    def share_copy(part, to):
        return pltpu.make_async_remote_copy(
            src_ref=end_grad.at[rows_of(me)],
            dst_ref=part_grads.at[part, rows_of(me)],
            send_sem=share_send.at[to],
            recv_sem=share_recv.at[part],
            device_id={"dp": to},
            device_id_type=MESH,
        )

    def spread_copy(part, source, to):
        return pltpu.make_async_remote_copy(
            src_ref=part_grads.at[part, rows_of(source)],
            dst_ref=part_grads.at[part, rows_of(source)],
            send_sem=spread_send.at[part, to // 2],
            recv_sem=spread_recv.at[part, source],
            device_id={"layer": to},
            device_id_type=MESH,
        )

    def odd_others(body):
        def step(i, _):
            to = 2 * i + 1

            @pl.when(to != me)
            def _():
                body(to)

            return 0

        lax.fori_loop(0, groups // 2, step, 0)

    other_planes(lambda to: share_copy(z, to).start(), me >= 0)

    line = (states_all, adj_all, part_images)
    piece = rows // count

    def line_copy(which, block, part, to, sends):
        where = line[which].at[block, part * piece : (part + 1) * piece]
        return pltpu.make_async_remote_copy(
            src_ref=where,
            dst_ref=where,
            send_sem=sends.at[which, block, part],
            recv_sem=line_recv.at[which, block, part],
            device_id={"dp": to},
            device_id_type=MESH,
        )

    def go_right(which, block, part):
        @pl.when(not_last)
        def _():
            line_copy(which, block, part, z + 1, right_send).start()

    def go_left(which, block, part):
        @pl.when(not_first)
        def _():
            line_copy(which, block, part, z - 1, left_send).start()

    def takes(which):
        return jnp.logical_not(lead) if which == 1 else lead

    def line_start(which):
        @pl.when(takes(which))
        def _():
            for part in range(count):
                go_right(which, z, part)
                go_left(which, z, part)

    def line_round(which, away, pieces=range(count)):
        for part in pieces:

            @pl.when(takes(which) & (z - away >= 0))
            def _():
                line_copy(which, z - away, part, z, right_send).wait_recv()
                go_right(which, z - away, part)

            @pl.when(takes(which) & (z + away < parts))
            def _():
                line_copy(which, z + away, part, z, left_send).wait_recv()
                go_left(which, z + away, part)

    line_start(2)

    def prepare(n, _):
        def tap(i, j):
            at = (3 * i + j) * channels
            return weights[n, at : at + channels, :]

        def spot(i):
            return slice(i * channels, (i + 1) * channels)

        nothing = jnp.zeros((channels, channels), low)
        for i in range(3):
            for j in range(2):
                ahead_pair[n, spot(j), spot(i)] = tap(i, j)
                back_pair[n, spot(i), spot(j)] = tap(2 - i, 2 - j)
        ahead_edge[n, spot(0), spot(0)] = tap(0, 2)
        ahead_edge[n, spot(0), spot(1)] = nothing
        ahead_edge[n, spot(1), spot(0)] = tap(1, 2)
        ahead_edge[n, spot(1), spot(1)] = tap(2, 2)
        back_edge[n, spot(0), spot(0)] = tap(2, 0)
        back_edge[n, spot(1), spot(0)] = nothing
        back_edge[n, spot(0), spot(1)] = tap(1, 0)
        back_edge[n, spot(1), spot(1)] = tap(0, 0)
        wg_out[n] = jnp.zeros(wg_out.shape[1:], jnp.float32)
        return 0

    lax.fori_loop(0, blocks, prepare, 0)
    bg_out[...] = jnp.zeros(bg_out.shape, jnp.float32)

    column = lax.rem(lax.broadcasted_iota(jnp.int32, (rows, channels), 0), width)

    area = height * width

    def down(field):
        blank = jnp.zeros((width, field.shape[1]), field.dtype)
        lines = []
        for at in range(0, field.shape[0], area):
            lines += [blank, field[at : at + area - width]]
        return jnp.concatenate(lines, axis=0)

    def up(field):
        blank = jnp.zeros((width, field.shape[1]), field.dtype)
        lines = []
        for at in range(0, field.shape[0], area):
            lines += [field[at + width : at + area], blank]
        return jnp.concatenate(lines, axis=0)

    def sides(field):
        size = field.shape[0]
        place = column[:size]
        left = jnp.where(place == 0, 0.0, pltpu.roll(field, 1, 0))
        right = jnp.where(place == width - 1, 0.0, pltpu.roll(field, size - 1, 0))
        return left.astype(low), field.astype(low), right.astype(low)

    def combine(three, pair_weights, edge_weights, contract):
        left, middle, right = three
        a = dot(jnp.concatenate([left, middle], axis=1), pair_weights, contract)
        b = dot(jnp.concatenate([down(right), right], axis=1), edge_weights, contract)
        c = channels
        return a[:, c : 2 * c] + b[:, :c] + down(a[:, :c]) + up(a[:, 2 * c :] + b[:, c:])

    def conv(n, field):
        return combine(sides(field), ahead_pair[n], ahead_edge[n], NN)

    def apply_map(field, slot, table=maps):
        return field + dot(field.astype(low), table[slot].astype(low))

    def apply_flipped(field, slot, table=maps):
        return field + dot(field.astype(low), table[slot].astype(low), NT)

    def split(field):
        return tuple(field[at : at + area] for at in range(0, field.shape[0], area))

    def join(fields):
        return jnp.concatenate(fields, axis=0)

    def span(i):
        return slice(i * area, (i + 1) * area)

    def advance(n, states):
        return tuple(
            state + step_size * jnp.tanh(conv(n, state) + biases[pl.ds(n, 1), :]) for state in states
        )

    def trajectory(part, state):
        def step(n, states):
            after = []
            for i, state in enumerate(states):
                states_low[n, part, span(i)] = state.astype(low)
                activation = jnp.tanh(conv(n, state) + biases[pl.ds(n, 1), :])
                slopes[n, part, span(i)] = activation
                after.append(state + step_size * activation)
            return tuple(after)

        return join(lax.fori_loop(0, blocks, step, split(state), unroll=4))

    def change_of(n, part, adjoint, i):
        slope = slopes[n, part, span(i)]
        return step_size * (1.0 - slope * slope) * adjoint

    def retreat(part, adjoint):
        def step(i, adjoints):
            n = blocks - 1 - i
            return tuple(
                adjoint + combine(sides(change_of(n, part, adjoint, at)), back_pair[n], back_edge[n], NT)
                for at, adjoint in enumerate(adjoints)
            )

        return join(lax.fori_loop(0, blocks, step, split(adjoint), unroll=4))

    divisor = 1.0 / images_all

    def sweep(part, adjoint, first=0):
        def step(i, adjoints):
            n = blocks - 1 - i
            after = []
            spots = []
            for at, adjoint in enumerate(adjoints):
                change = change_of(n, part, adjoint, first + at)
                bg_out[pl.ds(n, 1), :] += jnp.sum(change, axis=0, keepdims=True) * divisor
                three = sides(change)
                after.append(adjoint + combine(three, back_pair[n], back_edge[n], NT))
                line = jnp.concatenate(three, axis=1)
                spots.append(jnp.concatenate([down(line), line, up(line)], axis=1))
            used = states_low[n, part, first * area : (first + len(spots)) * area]
            grads = dot(used, join(spots), TN) * divisor
            for tap in range(9):
                wg_out[n, (8 - tap) * channels : (9 - tap) * channels, :] += grads[
                    :, tap * channels : (tap + 1) * channels
                ]
            return tuple(after)

        return join(lax.fori_loop(0, blocks, step, split(adjoint), unroll=4))

    def out_copy(phase, source, to):
        return pltpu.make_async_remote_copy(
            src_ref=residue.at[phase, rows_of(to)],
            dst_ref=gathered.at[phase, source],
            send_sem=out_send.at[phase, to],
            recv_sem=out_recv.at[phase, source],
            device_id={"layer": to},
            device_id_type=MESH,
        )

    def back_copy(phase, source, to):
        return pltpu.make_async_remote_copy(
            src_ref=spread.at[phase, to // 2],
            dst_ref=error.at[phase, rows_of(source)],
            send_sem=back_send.at[phase, to],
            recv_sem=back_recv.at[phase, source],
            device_id={"layer": to},
            device_id_type=MESH,
        )

    def lend_copy(phase):
        return pltpu.make_async_remote_copy(
            src_ref=raw,
            dst_ref=lent.at[phase],
            send_sem=lend_send.at[phase],
            recv_sem=lend_recv.at[phase],
            device_id={"layer": partner},
            device_id_type=MESH,
        )

    steps = (apply_map, apply_flipped)
    first_pair = (0, pairs - 1)

    def chain_start(phase, value):
        leads = takes(phase)

        @pl.when(leads)
        def _():
            residue[phase] = steps[phase](value, partner)

        @pl.when(jnp.logical_not(leads))
        def _():
            residue[phase] = value

        @pl.when(mine != first_pair[1 - phase])
        def _():
            others(lambda ahead, to: out_copy(phase, me, to).start())

        gathered[phase, me] = residue[phase, rows_of(me)]

        @pl.when(leads)
        def _():
            raw[...] = value
            lend_copy(phase).start()

    def chain_scan(phase):
        def deliver(m, value):
            spread[phase, m] = value

            for k in (2 * m, 2 * m + 1):

                @pl.when(k != me)
                def _():
                    back_copy(phase, me, k).start()

            @pl.when(m == mine)
            def _():
                error[phase, rows_of(me)] = value

        def both(m):
            for k in (2 * m, 2 * m + 1):

                @pl.when(k != me)
                def _():
                    out_copy(phase, k, me).wait_recv()

            return gathered[phase, 2 * m] + gathered[phase, 2 * m + 1]

        def pair_of(i):
            return i if phase == 0 else pairs - 1 - i

        def step(i, carried):
            m = pair_of(i)
            deliver(m, carried)
            moved = steps[phase](carried, m, pair_maps)
            return moved + both(m)

        carried = lax.fori_loop(1, pairs - 1, step, both(pair_of(0)))
        deliver(pair_of(pairs - 1), carried)

    def chain_finish(phase):
        @pl.when(mine != first_pair[phase])
        def _():
            others(lambda ahead, to: back_copy(phase, to, me).wait_recv())

        leads = takes(phase)

        @pl.when(jnp.logical_not(leads))
        def _():
            lend_copy(phase).wait_recv()

        value = jnp.where(mine == first_pair[phase], 0.0, error[phase])
        return jnp.where(leads, value, steps[phase](value, partner) + lent[phase])

    def nth_other(i):
        back_side = parts - 1 - z
        paired = jnp.where(z < back_side, z, back_side)
        near = i // 2 + 1
        outward = jnp.where(z > back_side, near, -near)
        near_part = jnp.where(i % 2 == 0, z + outward, z - outward)
        far = i - paired + 1
        far_part = jnp.where(z > back_side, z - far, z + far)
        return jnp.where(i < 2 * paired, near_part, far_part)

    def start_of(field):
        return jnp.where(me == 0, field, apply_map(field, jnp.where(me == 0, me, before)))

    def relax(start):
        return join(lax.fori_loop(0, blocks, advance, split(start), unroll=4))

    def relax_other(i):
        @pl.when(lead)
        def _():
            part = nth_other(i)
            start = start_of(part_images[part])
            other_starts[part] = start
            other_fine[part] = relax(start)

    def share_on(i):
        part = nth_other(i)
        share_copy(part, z).wait_recv()
        odd_others(lambda to: spread_copy(part, me, to).start())

    def retreat_other(i):
        @pl.when(jnp.logical_not(lead))
        def _():
            part = nth_other(i)
            others(lambda ahead, source: spread_copy(part, source, me).wait_recv())
            cotangent = ends_of(part_grads[part])
            other_starts[part] = cotangent
            other_fine[part] = retreat(part, cotangent)

    def pass_copy(which, part, i):
        where = pl.ds(i * piece, piece)
        return pltpu.make_async_remote_copy(
            src_ref=handoff.at[part, where],
            dst_ref=line[which].at[part, where],
            send_sem=pass_send.at[part, i],
            recv_sem=pass_recv.at[which, part, i],
            device_id={"layer": partner},
            device_id_type=MESH,
        )

    def pass_on(which, i, pieces=range(count)):
        part = nth_other(i)
        apply = apply_map if which == 0 else apply_flipped

        @pl.when(takes(which))
        def _():
            for at in pieces:
                where = slice(at * piece, (at + 1) * piece)
                change = line[which][part, where] - other_starts[part, where]
                handoff[part, where] = apply(change, me) + other_fine[part, where]
                pass_copy(which, part, at).start()

    def pass_wait(which, i, pieces=range(count)):
        part = nth_other(i)

        @pl.when(jnp.logical_not(takes(which)))
        def _():
            for at in pieces:
                pass_copy(which, part, at).wait_recv()

    def other_trajectory(i):
        part = nth_other(i)
        trajectory(part, states_all[part])

    start_image = part_images[z]

    def wait_before():
        @pl.when(me > 0)
        def _():
            map_copy(before, me).wait_recv()

    def wait_after():
        @pl.when(me < last)
        def _():
            map_copy(after, me).wait_recv()

    def join_pair():
        one = maps[2 * mine]
        two = maps[2 * mine + 1]
        pair_maps[mine] = one + two + dot(one.astype(low), two.astype(low))

    @pl.when(jnp.logical_not(odd))
    def _():
        wait_after()
        join_pair()

    pair_sends(lambda copy: copy.start())
    wait_before()
    starts = start_of(start_image)
    chain_start(0, relax(starts) - apply_map(start_image, me))

    far_maps(lambda to: map_copy(me, to).start())

    @pl.when(odd)
    def _():
        join_pair()

    hand_pairs()

    def ends_of(field):
        return jnp.where(me == last, field, apply_flipped(field, after))

    others_count = parts - 1

    def images_on(i):
        if i < others_count:
            line_round(2, i + 1)

    def relax_on(i):
        if i < others_count:
            relax_other(i)

    def states_on(i):
        if i < others_count:
            line_round(0, i + 1)
            pass_on(0, i)

    def follow(i):
        if i < others_count:
            pass_wait(0, i)
            other_trajectory(i)

    def answer(i):
        if i < others_count:
            retreat_other(i)

    chain_scan(0)
    for i in range(others_count):
        share_on(i)
    images_on(0)
    relax_on(0)

    @pl.when(odd)
    def _():
        wait_after()

    end = end_grad[...]
    ends_adj = ends_of(end)
    back = apply_flipped(end, me)
    corrected = starts + chain_finish(0)
    states_all[z] = corrected
    line_start(0)
    both_out[0] = trajectory(z, corrected)

    chain_start(1, retreat(z, ends_adj) - back)
    images_on(1)
    relax_on(1)
    states_on(0)
    follow(0)
    chain_scan(1)
    answer(0)
    images_on(2)
    relax_on(2)
    states_on(1)
    follow(1)
    adjoint = ends_adj + chain_finish(1)
    adj_all[z] = adjoint
    line_start(1)
    for i in range(2, others_count):
        if i > 2:
            images_on(i)
            relax_on(i)
        states_on(i)
    both_out[1] = sweep(z, adjoint)
    for i in range(2, others_count):
        follow(i)
    early = range(count // 2)
    late = range(count // 2, count)
    if parts > 1:
        line_round(1, 1, early)
        pass_on(1, 0, early)
        answer(1)
    for i in range(others_count):
        line_round(1, i + 1, late)
        pass_on(1, i, late)
        part = nth_other(i)
        if i < others_count - 1:
            pass_wait(1, i)
            sweep(part, adj_all[part])
            line_round(1, i + 2, early)
            pass_on(1, i + 1, early)
            answer(i + 2)
        else:

            @pl.when(jnp.logical_not(lead))
            def _():
                sweep(part, adj_all[part])

            @pl.when(lead)
            def _():
                for at in range(count):
                    pass_wait(1, i, (at,))
                    sweep(part, adj_all[part, at * piece : (at + 1) * piece], at)

    near_maps(lambda to: map_copy(me, to).wait_send())
    far_maps(lambda to: map_copy(me, to).wait_send())
    pair_sends(lambda copy: copy.wait_send())

    @pl.when(jnp.logical_not(odd))
    def _():
        other_pairs(lambda m: pair_copy(m, partner, hand_send.at[m]).wait_send())

    for phase in range(2):

        @pl.when(takes(phase))
        def _():
            lend_copy(phase).wait_send()

    def sent(ahead, to):
        for phase in range(2):

            @pl.when(mine != first_pair[1 - phase])
            def _():
                out_copy(phase, me, to).wait_send()

            @pl.when(to // 2 != first_pair[phase])
            def _():
                back_copy(phase, me, to).wait_send()

    others(sent)
    for which in range(3):
        for away in range(parts):

            @pl.when(takes(which) & (z - away >= 0) & not_last)
            def _():
                for part in range(count):
                    line_copy(which, z - away, part, z + 1, right_send).wait_send()

            @pl.when(takes(which) & (z + away < parts) & not_first)
            def _():
                for part in range(count):
                    line_copy(which, z + away, part, z - 1, left_send).wait_send()

    other_planes(lambda to: share_copy(z, to).wait_send(), me >= 0)

    def passed(part):
        for i in range(count):
            for which in range(2):

                @pl.when(takes(which))
                def _():
                    pass_copy(which, part, i).wait_send()

        odd_others(lambda to: spread_copy(part, me, to).wait_send())

    other_planes(passed, me >= 0)


def write_out(both, wg, bg, ends_out, starts_out, wg_out, bg_out, sems):
    copies = [
        pltpu.make_async_copy(source, target, sems.at[i])
        for i, (source, target) in enumerate(
            ((wg, wg_out), (both.at[0], ends_out), (both.at[1], starts_out), (bg, bg_out))
        )
    ]
    for copy in copies:
        copy.start()
    for copy in copies:
        copy.wait()


def shards(images, weights, biases, end_grad):
    groups = lax.axis_size("layer")
    parts = lax.axis_size("dp")
    count, height, width, channels = images.shape
    blocks = weights.shape[0]
    rows = count * height * width
    dims = (groups, parts, count, height, width, count * parts)
    f32 = jnp.float32
    share = rows // groups
    dma = pltpu.SemaphoreType.DMA
    vmem = pl.BlockSpec(memory_space=pltpu.VMEM)
    both, wg, bg = pl.pallas_call(
        functools.partial(kernel, dims),
        out_shape=(
            pltpu.VMEM((2, rows, channels), f32),
            pltpu.VMEM((blocks, 9 * channels, channels), f32),
            pltpu.VMEM((blocks, channels), f32),
        ),
        in_specs=[pl.BlockSpec(memory_space=pltpu.HBM)] * 4,
        out_specs=(vmem,) * 3,
        scratch_shapes=[
            pltpu.VMEM((blocks, 9 * channels, channels), low),
            pltpu.VMEM((blocks, channels), f32),
            pltpu.VMEM((rows, channels), f32),
            dma((4,)),
            pltpu.VMEM((blocks, 2 * channels, 3 * channels), low),
            pltpu.VMEM((blocks, 2 * channels, 2 * channels), low),
            pltpu.VMEM((blocks, 3 * channels, 2 * channels), low),
            pltpu.VMEM((blocks, 2 * channels, 2 * channels), low),
            pltpu.VMEM((groups, channels, channels), f32),
            pltpu.VMEM((blocks, parts, rows, channels), low),
            pltpu.VMEM((blocks, parts, rows, channels), f32),
            pltpu.VMEM((parts, rows, channels), f32),
            pltpu.VMEM((parts, rows, channels), f32),
            pltpu.VMEM((2, rows, channels), f32),
            pltpu.VMEM((2, groups, share, channels), f32),
            pltpu.VMEM((2, groups, share, channels), f32),
            pltpu.VMEM((2, rows, channels), f32),
            dma((groups,)),
            dma((groups,)),
            dma((groups,)),
            dma((2, groups)),
            dma((2, groups)),
            dma((2, groups)),
            dma((2, groups)),
            dma((3, parts, count)),
            dma((3, parts, count)),
            dma((3, parts, count)),
            pltpu.VMEM((parts, rows, channels), f32),
            pltpu.VMEM((parts, rows, channels), f32),
            pltpu.VMEM((parts, rows, channels), f32),
            pltpu.VMEM((parts, rows, channels), f32),
            dma((parts, count)),
            dma((2, parts, count)),
            pltpu.VMEM((parts, rows, channels), f32),
            dma((parts,)),
            dma((parts,)),
            dma((parts, groups // 2)),
            dma((parts, groups)),
            pltpu.VMEM((groups // 2, channels, channels), f32),
            dma((groups // 2,)),
            dma((groups // 2,)),
            pltpu.VMEM((rows, channels), f32),
            pltpu.VMEM((2, rows, channels), f32),
            dma((2,)),
            dma((2,)),
        ],
        compiler_params=pltpu.CompilerParams(
            collective_id=0, has_side_effects=True, vmem_limit_bytes=61 << 20
        ),
    )(
        images.reshape(rows, channels),
        weights.reshape(blocks, 9 * channels, channels),
        biases,
        end_grad.reshape(rows, channels),
    )
    shape = (1,) + images.shape
    hbm = pl.BlockSpec(memory_space=pltpu.HBM)
    ends, starts, wg, bg = pl.pallas_call(
        write_out,
        out_shape=(
            jax.ShapeDtypeStruct((rows, channels), f32),
            jax.ShapeDtypeStruct((rows, channels), f32),
            jax.ShapeDtypeStruct((blocks, 9 * channels, channels), f32),
            jax.ShapeDtypeStruct((blocks, channels), f32),
        ),
        in_specs=[vmem] * 3,
        out_specs=(hbm,) * 4,
        scratch_shapes=[dma((4,))],
        compiler_params=pltpu.CompilerParams(vmem_limit_bytes=1 << 20),
    )(*(pltpu.with_memory_space_constraint(x, pltpu.VMEM) for x in (both, wg, bg)))
    return (ends.reshape(shape), starts.reshape(shape), wg.reshape(weights.shape), bg)


def solution(mesh):
    in_specs = (
        P("dp", None, None, None),
        P("layer", None, None, None, None),
        P("layer", None),
        P("dp", None, None, None),
    )
    out_specs = (
        P("layer", "dp", None, None, None),
        P("layer", "dp", None, None, None),
        P("layer", None, None, None, None),
        P("layer", None),
    )
    return jax.shard_map(shards, mesh=mesh, in_specs=in_specs, out_specs=out_specs, check_vma=False)
```

```python
import functools

import jax
import jax.numpy as jnp
from jax import lax
from jax.experimental import pallas as pl
from jax.experimental.pallas import tpu as pltpu
from jax.sharding import PartitionSpec as P

step_size = 0.25
MESH = pl.DeviceIdType.MESH
low = jnp.bfloat16


def dot(a, b, contract=((1,), (0,))):
    return lax.dot_general(a, b, (contract, ((), ())), preferred_element_type=jnp.float32)


NN = ((1,), (0,))
NT = ((1,), (1,))
TN = ((0,), (0,))


def kernel(
    dims,
    images_in,
    weights_in,
    biases_in,
    end_grad_in,
    both_out,
    wg_out,
    bg_out,
    weights,
    biases,
    end_grad,
    load_sems,
    ahead_pair,
    ahead_edge,
    back_pair,
    back_edge,
    maps,
    states_low,
    slopes,
    states_all,
    adj_all,
    residue,
    gathered,
    spread,
    error,
    map_send,
    map_recv,
    hand_send,
    out_send,
    out_recv,
    back_send,
    back_recv,
    right_send,
    left_send,
    line_recv,
    part_images,
    other_starts,
    other_fine,
    handoff,
    pass_send,
    pass_recv,
    part_grads,
    share_send,
    share_recv,
    spread_send,
    spread_recv,
    pair_maps,
    pair_send,
    pair_recv,
    raw,
    lent,
    lend_send,
    lend_recv,
):
    groups, parts, count, height, width, images_all = dims
    rows, channels = images_in.shape
    blocks = weights_in.shape[0]
    share = rows // groups
    me = lax.axis_index("layer")
    z = lax.axis_index("dp")
    not_first = z > 0
    not_last = z < parts - 1

    def others(body):
        def step(ahead, _):
            body(ahead, lax.rem(me + ahead, groups))
            return 0

        lax.fori_loop(1, groups, step, 0)

    loads = [
        pltpu.make_async_copy(source, target, load_sems.at[i])
        for i, (source, target) in enumerate(
            ((weights_in, weights), (images_in, part_images.at[z]), (biases_in, biases), (end_grad_in, end_grad))
        )
    ]
    for load in loads:
        load.start()
    barrier = pltpu.get_barrier_semaphore()
    others(lambda ahead, to: pl.semaphore_signal(barrier, inc=1, device_id={"layer": to}, device_id_type=MESH))

    for ahead in range(1, parts):
        pl.semaphore_signal(
            barrier, inc=1, device_id={"dp": lax.rem(z + ahead, parts)}, device_id_type=MESH
        )

    loads[0].wait()
    centre = slice(4 * channels, 5 * channels)
    total = weights[0, centre, :].astype(jnp.float32)
    for n in range(1, blocks):
        total = total + weights[n, centre, :].astype(jnp.float32)
    maps[me] = step_size * total

    pl.semaphore_wait(barrier, groups - 1 + parts - 1)

    def map_copy(slot, to):
        return pltpu.make_async_remote_copy(
            src_ref=maps.at[slot],
            dst_ref=maps.at[slot],
            send_sem=map_send.at[to],
            recv_sem=map_recv.at[slot],
            device_id={"layer": to},
            device_id_type=MESH,
        )

    last = groups - 1
    after = jnp.minimum(me + 1, last)
    before = jnp.maximum(me - 1, 0)
    partner = me + 1 - 2 * lax.rem(me, 2)
    inner = (me > 0) & (me < last)

    def same_side(body):
        def step(ahead, _):
            body(lax.rem(me + 2 * ahead, groups))
            return 0

        lax.fori_loop(1, groups // 2, step, 0)

    odd = lax.rem(me, 2) == 1
    pairs = groups // 2
    mine = me // 2

    def is_inner(m):
        return (m > 0) & (m < pairs - 1)

    def near_maps(body):
        @pl.when(me != partner)
        def _():
            body(partner)

        @pl.when(odd & (me < last))
        def _():
            body(after)

    def far_maps(body):
        @pl.when(jnp.logical_not(odd) & (me > 0))
        def _():
            body(before)

    near_maps(lambda to: map_copy(me, to).start())

    def pair_copy(m, to, sends):
        return pltpu.make_async_remote_copy(
            src_ref=pair_maps.at[m],
            dst_ref=pair_maps.at[m],
            send_sem=sends,
            recv_sem=pair_recv.at[m],
            device_id={"layer": to},
            device_id_type=MESH,
        )

    def pair_sends(body):
        @pl.when(jnp.logical_not(odd) & is_inner(mine))
        def _():
            same_side(lambda to: body(pair_copy(mine, to, pair_send.at[to // 2])))

    def other_pairs(body):
        def step(m, _):
            @pl.when(m != mine)
            def _():
                body(m)

            return 0

        lax.fori_loop(1, pairs - 1, step, 0)

    def hand_pairs():
        @pl.when(jnp.logical_not(odd))
        def _():
            def hand(m):
                pair_copy(m, me, pair_send.at[m]).wait_recv()
                pair_copy(m, partner, hand_send.at[m]).start()

            other_pairs(hand)

        @pl.when(odd)
        def _():
            other_pairs(lambda m: pair_copy(m, me, pair_send.at[m]).wait_recv())

    for load in loads[1:]:
        load.wait()

    lead = lax.rem(me, 2) == 0

    def rows_of(slot):
        return pl.ds(pl.multiple_of(slot * share, share), share)

    def other_planes(body, who=True):
        for away in range(1, parts):

            @pl.when(who & (z + away < parts))
            def _():
                body(z + away)

            @pl.when(who & (z - away >= 0))
            def _():
                body(z - away)

    def share_copy(part, to):
        return pltpu.make_async_remote_copy(
            src_ref=end_grad.at[rows_of(me)],
            dst_ref=part_grads.at[part, rows_of(me)],
            send_sem=share_send.at[to],
            recv_sem=share_recv.at[part],
            device_id={"dp": to},
            device_id_type=MESH,
        )

    def spread_copy(part, source, to):
        return pltpu.make_async_remote_copy(
            src_ref=part_grads.at[part, rows_of(source)],
            dst_ref=part_grads.at[part, rows_of(source)],
            send_sem=spread_send.at[part, to // 2],
            recv_sem=spread_recv.at[part, source],
            device_id={"layer": to},
            device_id_type=MESH,
        )

    def odd_others(body):
        def step(i, _):
            to = 2 * i + 1

            @pl.when(to != me)
            def _():
                body(to)

            return 0

        lax.fori_loop(0, groups // 2, step, 0)

    other_planes(lambda to: share_copy(z, to).start(), me >= 0)

    line = (states_all, adj_all, part_images)
    piece = rows // count

    def line_copy(which, block, part, to, sends):
        where = line[which].at[block, part * piece : (part + 1) * piece]
        return pltpu.make_async_remote_copy(
            src_ref=where,
            dst_ref=where,
            send_sem=sends.at[which, block, part],
            recv_sem=line_recv.at[which, block, part],
            device_id={"dp": to},
            device_id_type=MESH,
        )

    def go_right(which, block, part):
        @pl.when(not_last)
        def _():
            line_copy(which, block, part, z + 1, right_send).start()

    def go_left(which, block, part):
        @pl.when(not_first)
        def _():
            line_copy(which, block, part, z - 1, left_send).start()

    def takes(which):
        return jnp.logical_not(lead) if which == 1 else lead

    def line_start(which):
        @pl.when(takes(which))
        def _():
            for part in range(count):
                go_right(which, z, part)
                go_left(which, z, part)

    def line_round(which, away, pieces=range(count)):
        for part in pieces:

            @pl.when(takes(which) & (z - away >= 0))
            def _():
                line_copy(which, z - away, part, z, right_send).wait_recv()
                go_right(which, z - away, part)

            @pl.when(takes(which) & (z + away < parts))
            def _():
                line_copy(which, z + away, part, z, left_send).wait_recv()
                go_left(which, z + away, part)

    line_start(2)

    def prepare(n, _):
        def tap(i, j):
            at = (3 * i + j) * channels
            return weights[n, at : at + channels, :]

        def spot(i):
            return slice(i * channels, (i + 1) * channels)

        nothing = jnp.zeros((channels, channels), low)
        for i in range(3):
            for j in range(2):
                ahead_pair[n, spot(j), spot(i)] = tap(i, j)
                back_pair[n, spot(i), spot(j)] = tap(2 - i, 2 - j)
        ahead_edge[n, spot(0), spot(0)] = tap(0, 2)
        ahead_edge[n, spot(0), spot(1)] = nothing
        ahead_edge[n, spot(1), spot(0)] = tap(1, 2)
        ahead_edge[n, spot(1), spot(1)] = tap(2, 2)
        back_edge[n, spot(0), spot(0)] = tap(2, 0)
        back_edge[n, spot(1), spot(0)] = nothing
        back_edge[n, spot(0), spot(1)] = tap(1, 0)
        back_edge[n, spot(1), spot(1)] = tap(0, 0)
        return 0

    lax.fori_loop(0, blocks, prepare, 0)
    bg_out[...] = jnp.zeros(bg_out.shape, jnp.float32)

    column = lax.rem(lax.broadcasted_iota(jnp.int32, (rows, channels), 0), width)

    area = height * width

    def down(field):
        blank = jnp.zeros((width, field.shape[1]), field.dtype)
        lines = []
        for at in range(0, field.shape[0], area):
            lines += [blank, field[at : at + area - width]]
        return jnp.concatenate(lines, axis=0)

    def up(field):
        blank = jnp.zeros((width, field.shape[1]), field.dtype)
        lines = []
        for at in range(0, field.shape[0], area):
            lines += [field[at + width : at + area], blank]
        return jnp.concatenate(lines, axis=0)

    def sides(field):
        size = field.shape[0]
        place = column[:size]
        left = jnp.where(place == 0, 0.0, pltpu.roll(field, 1, 0))
        right = jnp.where(place == width - 1, 0.0, pltpu.roll(field, size - 1, 0))
        return left.astype(low), field.astype(low), right.astype(low)

    def combine(three, pair_weights, edge_weights, contract):
        left, middle, right = three
        a = dot(jnp.concatenate([left, middle], axis=1), pair_weights, contract)
        b = dot(jnp.concatenate([down(right), right], axis=1), edge_weights, contract)
        c = channels
        return a[:, c : 2 * c] + b[:, :c] + down(a[:, :c]) + up(a[:, 2 * c :] + b[:, c:])

    def conv(n, field):
        return combine(sides(field), ahead_pair[n], ahead_edge[n], NN)

    def apply_map(field, slot, table=maps):
        return field + dot(field.astype(low), table[slot].astype(low))

    def apply_flipped(field, slot, table=maps):
        return field + dot(field.astype(low), table[slot].astype(low), NT)

    def split(field):
        return tuple(field[at : at + area] for at in range(0, field.shape[0], area))

    def join(fields):
        return jnp.concatenate(fields, axis=0)

    def span(i):
        return slice(i * area, (i + 1) * area)

    def advance(n, states):
        return tuple(
            state + step_size * jnp.tanh(conv(n, state) + biases[pl.ds(n, 1), :]) for state in states
        )

    def trajectory(part, state):
        def step(n, states):
            after = []
            for i, state in enumerate(states):
                states_low[n, part, span(i)] = state.astype(low)
                activation = jnp.tanh(conv(n, state) + biases[pl.ds(n, 1), :])
                slopes[n, part, span(i)] = activation
                after.append(state + step_size * activation)
            return tuple(after)

        return join(lax.fori_loop(0, blocks, step, split(state), unroll=4))

    def change_of(n, part, adjoint, i):
        slope = slopes[n, part, span(i)]
        return step_size * (1.0 - slope * slope) * adjoint

    def retreat(part, adjoint):
        def step(i, adjoints):
            n = blocks - 1 - i
            return tuple(
                adjoint + combine(sides(change_of(n, part, adjoint, at)), back_pair[n], back_edge[n], NT)
                for at, adjoint in enumerate(adjoints)
            )

        return join(lax.fori_loop(0, blocks, step, split(adjoint), unroll=4))

    divisor = 1.0 / images_all

    def sweep(part, adjoint, first=0, fresh=False):
        def step(i, adjoints):
            n = blocks - 1 - i
            after = []
            spots = []
            for at, adjoint in enumerate(adjoints):
                change = change_of(n, part, adjoint, first + at)
                bg_out[pl.ds(n, 1), :] += jnp.sum(change, axis=0, keepdims=True) * divisor
                three = sides(change)
                after.append(adjoint + combine(three, back_pair[n], back_edge[n], NT))
                line = jnp.concatenate(three, axis=1)
                spots.append(jnp.concatenate([down(line), line, up(line)], axis=1))
            used = states_low[n, part, first * area : (first + len(spots)) * area]
            grads = dot(used, join(spots), TN) * divisor
            for tap in range(9):
                place = slice((8 - tap) * channels, (9 - tap) * channels)
                grad = grads[:, tap * channels : (tap + 1) * channels]
                wg_out[n, place, :] = grad if fresh else wg_out[n, place, :] + grad
            return tuple(after)

        return join(lax.fori_loop(0, blocks, step, split(adjoint), unroll=4))

    def out_copy(phase, source, to):
        return pltpu.make_async_remote_copy(
            src_ref=residue.at[phase, rows_of(to)],
            dst_ref=gathered.at[phase, source],
            send_sem=out_send.at[phase, to],
            recv_sem=out_recv.at[phase, source],
            device_id={"layer": to},
            device_id_type=MESH,
        )

    def back_copy(phase, source, to):
        return pltpu.make_async_remote_copy(
            src_ref=spread.at[phase, to // 2],
            dst_ref=error.at[phase, rows_of(source)],
            send_sem=back_send.at[phase, to],
            recv_sem=back_recv.at[phase, source],
            device_id={"layer": to},
            device_id_type=MESH,
        )

    def lend_copy(phase):
        return pltpu.make_async_remote_copy(
            src_ref=raw,
            dst_ref=lent.at[phase],
            send_sem=lend_send.at[phase],
            recv_sem=lend_recv.at[phase],
            device_id={"layer": partner},
            device_id_type=MESH,
        )

    steps = (apply_map, apply_flipped)
    first_pair = (0, pairs - 1)

    def chain_start(phase, value):
        leads = takes(phase)

        @pl.when(leads)
        def _():
            residue[phase] = steps[phase](value, partner)

        @pl.when(jnp.logical_not(leads))
        def _():
            residue[phase] = value

        @pl.when(mine != first_pair[1 - phase])
        def _():
            others(lambda ahead, to: out_copy(phase, me, to).start())

        gathered[phase, me] = residue[phase, rows_of(me)]

        @pl.when(leads)
        def _():
            raw[...] = value
            lend_copy(phase).start()

    def chain_scan(phase):
        def deliver(m, value):
            spread[phase, m] = value

            for k in (2 * m, 2 * m + 1):

                @pl.when(k != me)
                def _():
                    back_copy(phase, me, k).start()

            @pl.when(m == mine)
            def _():
                error[phase, rows_of(me)] = value

        def both(m):
            for k in (2 * m, 2 * m + 1):

                @pl.when(k != me)
                def _():
                    out_copy(phase, k, me).wait_recv()

            return gathered[phase, 2 * m] + gathered[phase, 2 * m + 1]

        def pair_of(i):
            return i if phase == 0 else pairs - 1 - i

        def step(i, carried):
            m = pair_of(i)
            deliver(m, carried)
            moved = steps[phase](carried, m, pair_maps)
            return moved + both(m)

        carried = lax.fori_loop(1, pairs - 1, step, both(pair_of(0)))
        deliver(pair_of(pairs - 1), carried)

    def chain_finish(phase):
        @pl.when(mine != first_pair[phase])
        def _():
            others(lambda ahead, to: back_copy(phase, to, me).wait_recv())

        leads = takes(phase)

        @pl.when(jnp.logical_not(leads))
        def _():
            lend_copy(phase).wait_recv()

        value = jnp.where(mine == first_pair[phase], 0.0, error[phase])
        return jnp.where(leads, value, steps[phase](value, partner) + lent[phase])

    def nth_other(i):
        back_side = parts - 1 - z
        paired = jnp.where(z < back_side, z, back_side)
        near = i // 2 + 1
        outward = jnp.where(z > back_side, near, -near)
        near_part = jnp.where(i % 2 == 0, z + outward, z - outward)
        far = i - paired + 1
        far_part = jnp.where(z > back_side, z - far, z + far)
        return jnp.where(i < 2 * paired, near_part, far_part)

    def start_of(field):
        return jnp.where(me == 0, field, apply_map(field, jnp.where(me == 0, me, before)))

    def relax(start):
        return join(lax.fori_loop(0, blocks, advance, split(start), unroll=4))

    def relax_other(i):
        @pl.when(lead)
        def _():
            part = nth_other(i)
            start = start_of(part_images[part])
            other_starts[part] = start
            other_fine[part] = relax(start)

    def share_on(i):
        part = nth_other(i)
        share_copy(part, z).wait_recv()
        odd_others(lambda to: spread_copy(part, me, to).start())

    def retreat_other(i):
        @pl.when(jnp.logical_not(lead))
        def _():
            part = nth_other(i)
            others(lambda ahead, source: spread_copy(part, source, me).wait_recv())
            cotangent = ends_of(part_grads[part])
            other_starts[part] = cotangent
            other_fine[part] = retreat(part, cotangent)

    def pass_copy(which, part, i):
        where = pl.ds(i * piece, piece)
        return pltpu.make_async_remote_copy(
            src_ref=handoff.at[part, where],
            dst_ref=line[which].at[part, where],
            send_sem=pass_send.at[part, i],
            recv_sem=pass_recv.at[which, part, i],
            device_id={"layer": partner},
            device_id_type=MESH,
        )

    def pass_on(which, i, pieces=range(count)):
        part = nth_other(i)
        apply = apply_map if which == 0 else apply_flipped

        @pl.when(takes(which))
        def _():
            for at in pieces:
                where = slice(at * piece, (at + 1) * piece)
                change = line[which][part, where] - other_starts[part, where]
                handoff[part, where] = apply(change, me) + other_fine[part, where]
                pass_copy(which, part, at).start()

    def pass_wait(which, i, pieces=range(count)):
        part = nth_other(i)

        @pl.when(jnp.logical_not(takes(which)))
        def _():
            for at in pieces:
                pass_copy(which, part, at).wait_recv()

    def other_trajectory(i):
        part = nth_other(i)
        trajectory(part, states_all[part])

    start_image = part_images[z]

    def wait_before():
        @pl.when(me > 0)
        def _():
            map_copy(before, me).wait_recv()

    def wait_after():
        @pl.when(me < last)
        def _():
            map_copy(after, me).wait_recv()

    def join_pair():
        one = maps[2 * mine]
        two = maps[2 * mine + 1]
        pair_maps[mine] = one + two + dot(one.astype(low), two.astype(low))

    @pl.when(jnp.logical_not(odd))
    def _():
        wait_after()
        join_pair()

    pair_sends(lambda copy: copy.start())
    wait_before()
    starts = start_of(start_image)
    chain_start(0, relax(starts) - apply_map(start_image, me))

    far_maps(lambda to: map_copy(me, to).start())

    @pl.when(odd)
    def _():
        join_pair()

    hand_pairs()

    def ends_of(field):
        return jnp.where(me == last, field, apply_flipped(field, after))

    others_count = parts - 1

    def images_on(i):
        if i < others_count:
            line_round(2, i + 1)

    def relax_on(i):
        if i < others_count:
            relax_other(i)

    def states_on(i):
        if i < others_count:
            line_round(0, i + 1)
            pass_on(0, i)

    def follow(i):
        if i < others_count:
            pass_wait(0, i)
            other_trajectory(i)

    def answer(i):
        if i < others_count:
            retreat_other(i)

    chain_scan(0)
    for i in range(others_count):
        share_on(i)
    images_on(0)
    relax_on(0)

    @pl.when(odd)
    def _():
        wait_after()

    end = end_grad[...]
    ends_adj = ends_of(end)
    back = apply_flipped(end, me)
    corrected = starts + chain_finish(0)
    states_all[z] = corrected
    line_start(0)
    both_out[0] = trajectory(z, corrected)

    chain_start(1, retreat(z, ends_adj) - back)
    images_on(1)
    relax_on(1)
    states_on(0)
    follow(0)
    chain_scan(1)
    answer(0)
    images_on(2)
    relax_on(2)
    states_on(1)
    follow(1)
    adjoint = ends_adj + chain_finish(1)
    adj_all[z] = adjoint
    line_start(1)
    for i in range(2, others_count):
        if i > 2:
            images_on(i)
            relax_on(i)
        states_on(i)
    both_out[1] = sweep(z, adjoint, fresh=True)
    for i in range(2, others_count):
        follow(i)
    early = range(count // 2)
    late = range(count // 2, count)
    if parts > 1:
        line_round(1, 1, early)
        pass_on(1, 0, early)
        answer(1)
    for i in range(others_count):
        line_round(1, i + 1, late)
        pass_on(1, i, late)
        part = nth_other(i)
        if i < others_count - 1:
            pass_wait(1, i)
            sweep(part, adj_all[part])
            line_round(1, i + 2, early)
            pass_on(1, i + 1, early)
            answer(i + 2)
        else:

            @pl.when(jnp.logical_not(lead))
            def _():
                sweep(part, adj_all[part])

            @pl.when(lead)
            def _():
                for at in range(count):
                    pass_wait(1, i, (at,))
                    sweep(part, adj_all[part, at * piece : (at + 1) * piece], at)

    near_maps(lambda to: map_copy(me, to).wait_send())
    far_maps(lambda to: map_copy(me, to).wait_send())
    pair_sends(lambda copy: copy.wait_send())

    @pl.when(jnp.logical_not(odd))
    def _():
        other_pairs(lambda m: pair_copy(m, partner, hand_send.at[m]).wait_send())

    for phase in range(2):

        @pl.when(takes(phase))
        def _():
            lend_copy(phase).wait_send()

    def sent(ahead, to):
        for phase in range(2):

            @pl.when(mine != first_pair[1 - phase])
            def _():
                out_copy(phase, me, to).wait_send()

            @pl.when(to // 2 != first_pair[phase])
            def _():
                back_copy(phase, me, to).wait_send()

    others(sent)
    for which in range(3):
        for away in range(parts):

            @pl.when(takes(which) & (z - away >= 0) & not_last)
            def _():
                for part in range(count):
                    line_copy(which, z - away, part, z + 1, right_send).wait_send()

            @pl.when(takes(which) & (z + away < parts) & not_first)
            def _():
                for part in range(count):
                    line_copy(which, z + away, part, z - 1, left_send).wait_send()

    other_planes(lambda to: share_copy(z, to).wait_send(), me >= 0)

    def passed(part):
        for i in range(count):
            for which in range(2):

                @pl.when(takes(which))
                def _():
                    pass_copy(which, part, i).wait_send()

        odd_others(lambda to: spread_copy(part, me, to).wait_send())

    other_planes(passed, me >= 0)


def write_out(both, wg, bg, ends_out, starts_out, wg_out, bg_out, sems):
    copies = [
        pltpu.make_async_copy(source, target, sems.at[i])
        for i, (source, target) in enumerate(
            ((wg, wg_out), (both.at[0], ends_out), (both.at[1], starts_out), (bg, bg_out))
        )
    ]
    for copy in copies:
        copy.start()
    for copy in copies:
        copy.wait()


def shards(images, weights, biases, end_grad):
    groups = lax.axis_size("layer")
    parts = lax.axis_size("dp")
    count, height, width, channels = images.shape
    blocks = weights.shape[0]
    rows = count * height * width
    dims = (groups, parts, count, height, width, count * parts)
    f32 = jnp.float32
    share = rows // groups
    dma = pltpu.SemaphoreType.DMA
    vmem = pl.BlockSpec(memory_space=pltpu.VMEM)
    both, wg, bg = pl.pallas_call(
        functools.partial(kernel, dims),
        out_shape=(
            pltpu.VMEM((2, rows, channels), f32),
            pltpu.VMEM((blocks, 9 * channels, channels), f32),
            pltpu.VMEM((blocks, channels), f32),
        ),
        in_specs=[pl.BlockSpec(memory_space=pltpu.HBM)] * 4,
        out_specs=(vmem,) * 3,
        scratch_shapes=[
            pltpu.VMEM((blocks, 9 * channels, channels), low),
            pltpu.VMEM((blocks, channels), f32),
            pltpu.VMEM((rows, channels), f32),
            dma((4,)),
            pltpu.VMEM((blocks, 2 * channels, 3 * channels), low),
            pltpu.VMEM((blocks, 2 * channels, 2 * channels), low),
            pltpu.VMEM((blocks, 3 * channels, 2 * channels), low),
            pltpu.VMEM((blocks, 2 * channels, 2 * channels), low),
            pltpu.VMEM((groups, channels, channels), f32),
            pltpu.VMEM((blocks, parts, rows, channels), low),
            pltpu.VMEM((blocks, parts, rows, channels), f32),
            pltpu.VMEM((parts, rows, channels), f32),
            pltpu.VMEM((parts, rows, channels), f32),
            pltpu.VMEM((2, rows, channels), f32),
            pltpu.VMEM((2, groups, share, channels), f32),
            pltpu.VMEM((2, groups, share, channels), f32),
            pltpu.VMEM((2, rows, channels), f32),
            dma((groups,)),
            dma((groups,)),
            dma((groups,)),
            dma((2, groups)),
            dma((2, groups)),
            dma((2, groups)),
            dma((2, groups)),
            dma((3, parts, count)),
            dma((3, parts, count)),
            dma((3, parts, count)),
            pltpu.VMEM((parts, rows, channels), f32),
            pltpu.VMEM((parts, rows, channels), f32),
            pltpu.VMEM((parts, rows, channels), f32),
            pltpu.VMEM((parts, rows, channels), f32),
            dma((parts, count)),
            dma((2, parts, count)),
            pltpu.VMEM((parts, rows, channels), f32),
            dma((parts,)),
            dma((parts,)),
            dma((parts, groups // 2)),
            dma((parts, groups)),
            pltpu.VMEM((groups // 2, channels, channels), f32),
            dma((groups // 2,)),
            dma((groups // 2,)),
            pltpu.VMEM((rows, channels), f32),
            pltpu.VMEM((2, rows, channels), f32),
            dma((2,)),
            dma((2,)),
        ],
        compiler_params=pltpu.CompilerParams(
            collective_id=0, has_side_effects=True, vmem_limit_bytes=61 << 20
        ),
    )(
        images.reshape(rows, channels),
        weights.reshape(blocks, 9 * channels, channels),
        biases,
        end_grad.reshape(rows, channels),
    )
    shape = (1,) + images.shape
    hbm = pl.BlockSpec(memory_space=pltpu.HBM)
    ends, starts, wg, bg = pl.pallas_call(
        write_out,
        out_shape=(
            jax.ShapeDtypeStruct((rows, channels), f32),
            jax.ShapeDtypeStruct((rows, channels), f32),
            jax.ShapeDtypeStruct((blocks, 9 * channels, channels), f32),
            jax.ShapeDtypeStruct((blocks, channels), f32),
        ),
        in_specs=[vmem] * 3,
        out_specs=(hbm,) * 4,
        scratch_shapes=[dma((4,))],
        compiler_params=pltpu.CompilerParams(vmem_limit_bytes=1 << 20),
    )(*(pltpu.with_memory_space_constraint(x, pltpu.VMEM) for x in (both, wg, bg)))
    return (ends.reshape(shape), starts.reshape(shape), wg.reshape(weights.shape), bg)


def solution(mesh):
    in_specs = (
        P("dp", None, None, None),
        P("layer", None, None, None, None),
        P("layer", None),
        P("dp", None, None, None),
    )
    out_specs = (
        P("layer", "dp", None, None, None),
        P("layer", "dp", None, None, None),
        P("layer", None, None, None, None),
        P("layer", None),
    )
    return jax.shard_map(shards, mesh=mesh, in_specs=in_specs, out_specs=out_specs, check_vma=False)
```
